256 devices in a mesh: leaf: 16 (over y, x), row: 16 (over z, core).
Axes of the slice: x: 4, y: 4, z: 8, core: 2. Of those that a mesh axis runs over, the one named last changes fastest.
Arguments:
- sigma_root: float32 [2048, 2048], P(None, 'row')
- linv_one: bfloat16 [16, 2048, 2048], P('leaf', None, 'row'), as said below
- panel_one: bfloat16 [16, 512, 2048], P('leaf', None, 'row'), may hold values from -1.25 to 1.25
- tiles_one: int32 [16, 4], replicated, may hold values from 0 to 15, as said below
- mask_one: int32 [16, 4, 16], P('leaf', None, 'row'), may hold values 0 or 1
- linv_two: bfloat16 [16, 2048, 2048], P('leaf', None, 'row'), as said below
- panel_two: bfloat16 [16, 512, 2048], P('leaf', None, 'row'), may hold values from -1.25 to 1.25
- tiles_two: int32 [16, 4], replicated, may hold values from 0 to 15, as said below
- mask_two: int32 [16, 4, 16], P('leaf', None, 'row'), may hold values 0 or 1
- parent: int32 [16], replicated, may hold values from 0 to 15
Outputs:
- sigma_one: float32 [16, 2048, 2048], P('leaf', None, 'row')
- cross_one: float32 [16, 512, 2048], P('leaf', None, 'row')
- sigma_two: float32 [16, 2048, 2048], P('leaf', None, 'row')
- cross_two: float32 [16, 512, 2048], P('leaf', None, 'row')
The draws below stay inside these ranges and needn't reach their ends.
Inputs may be any that keep to these rules, and one draw needn't show every extreme that they name: `tiles_one`: each row holds 4 different tile numbers in increasing order. `tiles_two`: each row holds 4 different tile numbers in increasing order. `linv_one`: each block is lower triangular with a positive diagonal. `sigma_root`: symmetric. `linv_two`: each block is lower triangular with a positive diagonal.
All inputs are finite; a program needn't handle non-finite values. No bound on the sum of `mask_one` or of `mask_two` on one device may be relied on, other than what follows from the above.
Results may differ from the reference program's by a relative error of at most 0.00045.
Values may be sent and summed in bfloat16 or wider, within the bound.
No kernel may reach another device: no remote copies, remote signals or barrier semaphores. Data moves between devices by JAX's collectives and lax.ppermute only.
A program may use at most 64 MiB of HBM per device.

```python
import math
import jax
import jax.numpy as jnp
from jax import lax

NS = 2048
TILE = 128
K = 4
P_SIZE = 16
NT = 16
KB = 512
N_LEAF = 16


def lower_inverse(key):
    key_noise, key_diag = jax.random.split(key)
    noise = jax.random.normal(key_noise, (NS, NS), jnp.float32) * (1.0 / math.sqrt(NS))
    index = jnp.arange(NS, dtype=jnp.int32)
    below = (index[:, None] > index[None, :]).astype(jnp.float32)
    diagonal = jax.random.uniform(key_diag, (NS,), jnp.float32, 0.6, 1.6)
    return (noise * below + jnp.diag(diagonal)).astype(jnp.bfloat16)


def tile_lists(key):
    row_keys = jax.random.split(key, P_SIZE)

    def one_row(row_key):
        return jnp.sort(jax.random.permutation(row_key, NT)[:K])
    return jax.vmap(one_row)(row_keys).astype(jnp.int32)


def draw_sigma_root(key, part):
    key_noise, key_diag = jax.random.split(jax.random.fold_in(key, 3), 2)
    noise = jax.random.normal(key_noise, (NS, NS), jnp.float32)
    symmetric = (noise + noise.T) * (0.35 / math.sqrt(NS))
    diagonal = jnp.exp(jax.random.uniform(key_diag, (NS,), jnp.float32, math.log(1.5), math.log(3.0)))
    result = symmetric + jnp.diag(diagonal)
    return result


def draw_linv_one(key, part):
    row_keys = jax.random.split(jax.random.fold_in(key, 5), P_SIZE)
    return jax.vmap(lower_inverse)(row_keys)


def draw_linv_two(key, part):
    row_keys = jax.random.split(jax.random.fold_in(key, 7), P_SIZE)
    return jax.vmap(lower_inverse)(row_keys)


def draw_tiles_one(key, part):
    return tile_lists(jax.random.fold_in(key, 11))


def draw_tiles_two(key, part):
    return tile_lists(jax.random.fold_in(key, 13))


def place_ends(values, stream_key, smallest, largest):
    place = [jax.random.randint(jax.random.fold_in(stream_key, axis), (), 0, length) for axis, length in enumerate(values.shape)]
    longest = values.shape.index(max(values.shape))
    neighbour = place[:longest] + [(place[longest] + 1) % values.shape[longest]] + place[longest + 1:]
    return values.at[tuple(place)].set(smallest).at[tuple(neighbour)].set(largest)


def steps_of(own_key, dims, shards, smallest, largest):
    factor_of = 1.0
    for dim, shards_of in shards:
        steps = jax.random.uniform(jax.random.fold_in(jax.random.fold_in(own_key, 6), dim), (shards_of,), jnp.float32, smallest / len(shards), largest / len(shards))
        factor_of = factor_of * jnp.repeat(jnp.exp(steps), dims[dim] // shards_of).reshape((-1,) + (1,) * (len(dims) - 1 - dim))
    return factor_of


def scatter_about(own_key, shape, spread, reach, shards=(), kind=jnp.bfloat16):
    values = jax.random.normal(own_key, shape, jnp.float32) * spread
    if len(shards) > 0:
        values = steps_of(own_key, shape, shards, -0.22, 0.18) * values
    return jnp.clip(values, min=-reach, max=reach).astype(kind)


def setup_inputs(seed: int = 0) -> dict:
    seeds = jax.random.split(jax.random.key(seed), 11)
    return {
        "sigma_root": draw_sigma_root(jax.random.fold_in(seeds[10], 71), 0),
        "linv_one": draw_linv_one(jax.random.fold_in(seeds[10], 71), 0),
        "panel_one": scatter_about(seeds[2], (P_SIZE, KB, NS), (2.0 / (K * TILE) ** 0.5), 1.25, ((0, 16), (2, 16))),
        "tiles_one": draw_tiles_one(jax.random.fold_in(seeds[10], 71), 0),
        "mask_one": place_ends((jax.random.randint(seeds[4], (P_SIZE, K, NT), 0, 4) < 3).astype(jnp.int32), jax.random.fold_in(seeds[4], 1), 0, 1),
        "linv_two": draw_linv_two(jax.random.fold_in(seeds[10], 71), 0),
        "panel_two": scatter_about(seeds[6], (P_SIZE, KB, NS), (2.0 / (K * TILE) ** 0.5), 1.25, ((0, 16), (2, 16))),
        "tiles_two": draw_tiles_two(jax.random.fold_in(seeds[10], 71), 0),
        "mask_two": place_ends((jax.random.randint(seeds[8], (P_SIZE, K, NT), 0, 4) < 3).astype(jnp.int32), jax.random.fold_in(seeds[8], 1), 0, 1),
        "parent": place_ends(jax.random.randint(seeds[9], (P_SIZE,), 0, N_LEAF), jax.random.fold_in(seeds[9], 1), 0, N_LEAF - 1).astype(jnp.int32),
    }


def pattern_rows(tile_list):
    offsets = jnp.arange(TILE, dtype=jnp.int32)
    return (tile_list[:, None].astype(jnp.int32) * TILE + offsets[None, :]).reshape(-1)


def expand_mask(tile_mask):
    return jnp.repeat(jnp.repeat(tile_mask, TILE, axis=0), TILE, axis=1)


def solve_block(ancestor, linv, panel, tile_list, tile_mask):
    row_list = pattern_rows(tile_list)
    select = jnp.take(jnp.take(ancestor, row_list, axis=0), row_list, axis=1)
    masked = panel * expand_mask(tile_mask).astype(jnp.bfloat16)
    upper_part = jnp.dot(masked, linv, preferred_element_type=jnp.float32)
    cross = -jnp.dot(select, upper_part, precision=lax.Precision.HIGHEST)
    linv_wide = linv.astype(jnp.float32)
    middle = linv_wide - jnp.dot(masked.astype(jnp.float32).T, cross, precision=lax.Precision.HIGHEST)
    sigma = jnp.dot(linv_wide.T, middle, precision=lax.Precision.HIGHEST)
    return sigma, cross


def reference(sigma_root, linv_one, panel_one, tiles_one, mask_one, linv_two, panel_two, tiles_two, mask_two, parent):
    def first_level(items):
        return solve_block(sigma_root, items[0], items[1], items[2], items[3])

    sigma_one, cross_one = lax.map(first_level, (linv_one, panel_one, tiles_one, mask_one))

    def second_level(items):
        ancestor = lax.dynamic_index_in_dim(sigma_one, items[4], 0, keepdims=False)
        return solve_block(ancestor, items[0], items[1], items[2], items[3])

    sigma_two, cross_two = lax.map(second_level, (linv_two, panel_two, tiles_two, mask_two, parent))
    return sigma_one, cross_one, sigma_two, cross_two
```

```python
import functools

import jax
import jax.numpy as jnp
from jax import lax
from jax.experimental import pallas as pl
from jax.experimental.pallas import tpu as pltpu
from jax.sharding import PartitionSpec as P

TILE = 128
BF = jnp.bfloat16
F32 = jnp.float32
VMEM_SPEC = pl.BlockSpec(memory_space=pltpu.VMEM)
SMEM_SPEC = pl.BlockSpec(memory_space=pltpu.SMEM)
HBM_SPEC = pl.BlockSpec(memory_space=pltpu.HBM)
VMEM_LIMIT = 40 << 20
SOLVE_LIMIT = 60 << 20
SENT = 3


def split(x):
    high = x.astype(BF)
    return high, (x - high.astype(F32)).astype(BF)


def dot(a, b):
    return jnp.dot(a, b, preferred_element_type=F32)


def sent_tiles(tiles_ref, block, row_id):
    count = tiles_ref.shape[1]
    place = jnp.int32(0)
    for a in range(1, count):
        place = jnp.where(tiles_ref[block, a] == row_id, jnp.int32(a), place)
    picks = []
    for j in range(SENT):
        index = place + j
        picks.append(tiles_ref[block, jnp.where(index >= count, index - count, index)])
    return picks


def pack_kernel(with_select, mask_ref, panel_ref, linv_ref, *rest):
    if with_select:
        tiles_ref, select_ref, out_ref = rest
    else:
        (out_ref,) = rest
    kb = panel_ref.shape[0]
    ns = linv_ref.shape[0]
    for a in range(kb // TILE):
        rows = pl.ds(a * TILE, TILE)
        weight = mask_ref[a, 0].astype(F32)
        out_ref[rows, :] = (panel_ref[rows, :].astype(F32) * weight).astype(BF)
    out_ref[pl.ds(kb, ns), :] = linv_ref[...]
    if with_select:
        picks = sent_tiles(tiles_ref, lax.axis_index("leaf"), lax.axis_index("row"))
        for j in range(SENT):
            start = pl.multiple_of(picks[j] * TILE, TILE)
            high, low = split(select_ref[pl.ds(start, TILE), :])
            out_ref[pl.ds(kb + ns + j * TILE, TILE), :] = high
            out_ref[pl.ds(kb + ns + (SENT + j) * TILE, TILE), :] = low


def pack(mask, panel, linv, tiles=None, select=None):
    kb, width = panel.shape
    ns = linv.shape[0]
    extra = 0 if select is None else 2 * SENT * TILE
    operands = [mask, panel, linv]
    in_specs = [SMEM_SPEC, VMEM_SPEC, VMEM_SPEC]
    if select is not None:
        operands += [tiles, select]
        in_specs += [SMEM_SPEC, VMEM_SPEC]
    return pl.pallas_call(
        functools.partial(pack_kernel, select is not None),
        out_shape=jax.ShapeDtypeStruct((kb + ns + extra, width), BF),
        in_specs=in_specs,
        out_specs=VMEM_SPEC,
        compiler_params=pltpu.CompilerParams(vmem_limit_bytes=VMEM_LIMIT),
        cost_estimate=pl.CostEstimate(
            flops=0, transcendentals=0, bytes_accessed=2 * 2 * (kb + ns + extra) * width
        ),
        name="pack",
    )(*operands)


def solve_kernel(
    first, blocks, kb, tiles_ref, gath_ref, own_ref, *rest
):
    if first:
        slot_ref, sigma_ref, cross_ref, slots_ref = rest[:4]
        lm, lv, raw, sh, sl, mt, lm_sem, s_sem, lv_sem, out_sem = rest[4:]
    else:
        ancestor_ref, sigma_ref, cross_ref = rest[:3]
        lm, lv, raw, sh, sl, mt, lm_sem, s_sem, lv_sem = rest[3:]
    ns = blocks * TILE
    wide = 2 * TILE
    pairs = blocks // 2
    k = kb // TILE
    leaf_id = lax.axis_index("leaf")
    copies = [pltpu.make_async_copy(gath_ref.at[:, pl.ds(0, kb), :], lm, lm_sem)]
    for b in range(k):
        tile = tiles_ref[leaf_id, b]
        if first:
            source = gath_ref.at[tile, pl.ds(kb + ns, 2 * SENT * TILE), :]
        else:
            source = ancestor_ref.at[tile]
        copies.append(pltpu.make_async_copy(source, raw.at[b], s_sem.at[b]))
    lv_copies = []
    for j in range(pairs):
        lv_copies.append(
            pltpu.make_async_copy(
                gath_ref.at[pl.ds(2 * j, 2), pl.ds(kb + wide * j, ns - wide * j), :],
                lv.at[pl.ds(2 * j, 2), pl.ds(wide * j, ns - wide * j), :],
                lv_sem.at[j],
            )
        )
    for copy in copies + lv_copies:
        copy.start()

    def panel(j):
        return jnp.concatenate([lm[2 * j], lm[2 * j + 1]], axis=1)

    copies[0].wait()
    upper = jnp.zeros((kb, TILE), F32)
    for j in range(pairs):
        upper = upper + dot(panel(j), own_ref[pl.ds(wide * j, wide), :])
    upper_high, upper_low = split(upper)
    for b in range(k):
        copies[1 + b].wait()
        for j in range(SENT):
            if first:
                high = raw[b, pl.ds(j * TILE, TILE), :]
                low = raw[b, pl.ds((SENT + j) * TILE, TILE), :]
            else:
                high, low = split(raw[b, pl.ds(j * TILE, TILE), :])
            a = (b + j) % k
            sh[pl.ds(a * TILE, TILE), pl.ds(b * TILE, TILE)] = high
            sl[pl.ds(a * TILE, TILE), pl.ds(b * TILE, TILE)] = low
            if j == 1:
                sh[pl.ds(b * TILE, TILE), pl.ds(a * TILE, TILE)] = high.astype(F32).T.astype(BF)
                sl[pl.ds(b * TILE, TILE), pl.ds(a * TILE, TILE)] = low.astype(F32).T.astype(BF)
    both = dot(sh[...], jnp.concatenate([upper_high, upper_low], axis=1))
    cross = -(both[:, :TILE] + both[:, TILE:] + dot(sl[...], upper_high))
    cross_ref[...] = cross
    cross_high, cross_low = split(cross.T)
    stacked = jnp.concatenate([cross_high, cross_low], axis=0)
    for j in range(pairs):
        rows = pl.ds(wide * j, wide)
        part = dot(stacked, panel(j))
        middle = own_ref[rows, :].astype(F32).T - (part[:TILE] + part[TILE:])
        middle_high, middle_low = split(middle)
        mt[pl.ds(0, TILE), rows] = middle_high
        mt[pl.ds(TILE, TILE), rows] = middle_low
    for j in range(pairs):
        lv_copies[j].wait()
        total = jnp.zeros((wide, wide), F32)
        for i in range(j, pairs):
            rows = pl.ds(wide * i, wide)
            total = total + dot(
                mt[:, rows], jnp.concatenate([lv[2 * j, rows, :], lv[2 * j + 1, rows, :]], axis=1)
            )
        sigma_ref[pl.ds(wide * j, wide), :] = (total[:TILE] + total[TILE:]).T
    if first:
        out_copies = []
        row_id = lax.axis_index("row")
        for p in range(slots_ref.shape[0]):
            picks = sent_tiles(slot_ref, p, row_id)
            for j in range(SENT):
                start = pl.multiple_of(picks[j] * TILE, TILE)
                out_copies.append(
                    pltpu.make_async_copy(
                        sigma_ref.at[pl.ds(start, TILE), :],
                        slots_ref.at[p, pl.ds(j * TILE, TILE), :],
                        out_sem.at[p * SENT + j],
                    )
                )
        for copy in out_copies:
            copy.start()
        for copy in out_copies:
            copy.wait()


def solve(tiles, gathered, own, kb, slot_tiles=None, ancestor=None):
    first = ancestor is None
    blocks = gathered.shape[0]
    ns, width = own.shape
    k = kb // TILE
    outs = [
        jax.ShapeDtypeStruct((ns, width), F32),
        jax.ShapeDtypeStruct((kb, width), F32),
    ]
    out_specs = [VMEM_SPEC, VMEM_SPEC]
    scratch = [
        pltpu.VMEM((blocks, kb, width), BF),
        pltpu.VMEM((blocks, ns, width), BF),
        pltpu.VMEM((k, 2 * SENT * TILE, width), BF)
        if first
        else pltpu.VMEM((k, SENT * TILE, width), F32),
        pltpu.VMEM((kb, kb), BF),
        pltpu.VMEM((kb, kb), BF),
        pltpu.VMEM((2 * TILE, ns), BF),
        pltpu.SemaphoreType.DMA,
        pltpu.SemaphoreType.DMA((k,)),
        pltpu.SemaphoreType.DMA((blocks // 2,)),
    ]
    operands = [tiles, gathered, own]
    in_specs = [SMEM_SPEC, HBM_SPEC, VMEM_SPEC]
    if first:
        operands.append(slot_tiles)
        in_specs.append(SMEM_SPEC)
        count = slot_tiles.shape[0]
        outs.append(jax.ShapeDtypeStruct((count, SENT * TILE, width), F32))
        out_specs.append(HBM_SPEC)
        scratch.append(pltpu.SemaphoreType.DMA((count * SENT,)))
    else:
        operands.append(ancestor)
        in_specs.append(HBM_SPEC)
    return pl.pallas_call(
        functools.partial(solve_kernel, first, blocks, kb),
        out_shape=outs,
        in_specs=in_specs,
        out_specs=out_specs,
        scratch_shapes=scratch,
        compiler_params=pltpu.CompilerParams(vmem_limit_bytes=SOLVE_LIMIT),
        cost_estimate=pl.CostEstimate(
            flops=4 * ns * ns * width, transcendentals=0, bytes_accessed=14 << 20
        ),
        name="solve_first" if first else "solve_second",
    )(*operands)


def body(
    sigma_root,
    linv_one,
    panel_one,
    tiles_one,
    mask_one,
    linv_two,
    panel_two,
    tiles_two,
    mask_two,
    parent,
):
    leaf_id = lax.axis_index("leaf")
    kb = panel_one.shape[1]
    source = lax.dynamic_index_in_dim(parent, leaf_id, 0, keepdims=False)
    packed_one = pack(mask_one[0], panel_one[0], linv_one[0], tiles_one, sigma_root)
    packed_two = pack(mask_two[0], panel_two[0], linv_two[0])
    gathered_one = lax.all_gather(packed_one, "row", axis=0)
    gathered_one, packed_two = lax.optimization_barrier((gathered_one, packed_two))
    gathered_two = lax.all_gather(packed_two, "row", axis=0)
    sigma_first, cross_first, slots = solve(
        tiles_one, gathered_one, linv_one[0], kb, slot_tiles=tiles_two
    )
    arrived = lax.all_to_all(slots, "leaf", split_axis=0, concat_axis=0, tiled=True)
    chosen = lax.dynamic_index_in_dim(arrived, source, 0, keepdims=False)
    chosen, gathered_two = lax.optimization_barrier((chosen, gathered_two))
    ancestor = lax.all_gather(chosen, "row", axis=0)
    sigma_second, cross_second = solve(
        tiles_two, gathered_two, linv_two[0], kb, ancestor=ancestor
    )
    return (sigma_first[None], cross_first[None], sigma_second[None], cross_second[None])


def solution(mesh):
    return jax.shard_map(
        body,
        mesh=mesh,
        in_specs=(
            P(None, "row"),
            P("leaf", None, "row"),
            P("leaf", None, "row"),
            P(),
            P("leaf", None, "row"),
            P("leaf", None, "row"),
            P("leaf", None, "row"),
            P(),
            P("leaf", None, "row"),
            P(),
        ),
        out_specs=(
            P("leaf", None, "row"),
            P("leaf", None, "row"),
            P("leaf", None, "row"),
            P("leaf", None, "row"),
        ),
        check_vma=False,
    )
```

```python
import functools

import jax
import jax.numpy as jnp
from jax import lax
from jax.experimental import pallas as pl
from jax.experimental.pallas import tpu as pltpu
from jax.sharding import PartitionSpec as P

TILE = 128
BF = jnp.bfloat16
F32 = jnp.float32
VMEM_SPEC = pl.BlockSpec(memory_space=pltpu.VMEM)
SMEM_SPEC = pl.BlockSpec(memory_space=pltpu.SMEM)
HBM_SPEC = pl.BlockSpec(memory_space=pltpu.HBM)
VMEM_LIMIT = 40 << 20
SOLVE_LIMIT = 60 << 20
SENT = 3
SCALES = 16
STEPS = 256.0
TOP = 32512.0


def split(x):
    high = x.astype(BF)
    return high, (x - high.astype(F32)).astype(BF)


def code_tile(x):
    peak = jnp.max(jnp.abs(x), axis=0, keepdims=True)
    code = jnp.clip(jnp.ceil(jnp.log2(peak) * STEPS), -110.0 * STEPS, 127.0 * STEPS)
    levels = jnp.round(x * (TOP / jnp.exp2(code * (1.0 / STEPS))))
    return levels.astype(jnp.int32), code


def dot(a, b):
    return jnp.dot(a, b, preferred_element_type=F32)


def sent_tiles(tiles_ref, block, row_id):
    count = tiles_ref.shape[1]
    place = jnp.int32(0)
    for a in range(1, count):
        place = jnp.where(tiles_ref[block, a] == row_id, jnp.int32(a), place)
    picks = []
    for j in range(SENT):
        index = place + j
        picks.append(tiles_ref[block, jnp.where(index >= count, index - count, index)])
    return picks


def pack_kernel(with_select, mask_ref, panel_ref, linv_ref, *rest):
    if with_select:
        tiles_ref, select_ref, out_ref = rest
    else:
        (out_ref,) = rest
    kb = panel_ref.shape[0]
    ns = linv_ref.shape[0]
    for a in range(kb // TILE):
        rows = pl.ds(a * TILE, TILE)
        weight = mask_ref[a, 0].astype(F32)
        out_ref[rows, :] = (panel_ref[rows, :].astype(F32) * weight).astype(BF)
    out_ref[pl.ds(kb, ns), :] = linv_ref[...]
    if with_select:
        picks = sent_tiles(tiles_ref, lax.axis_index("leaf"), lax.axis_index("row"))
        for j in range(SENT):
            start = pl.multiple_of(picks[j] * TILE, TILE)
            high, low = split(select_ref[pl.ds(start, TILE), :])
            out_ref[pl.ds(kb + ns + j * TILE, TILE), :] = high
            out_ref[pl.ds(kb + ns + (SENT + j) * TILE, TILE), :] = low


def pack(mask, panel, linv, tiles=None, select=None):
    kb, width = panel.shape
    ns = linv.shape[0]
    extra = 0 if select is None else 2 * SENT * TILE
    operands = [mask, panel, linv]
    in_specs = [SMEM_SPEC, VMEM_SPEC, VMEM_SPEC]
    if select is not None:
        operands += [tiles, select]
        in_specs += [SMEM_SPEC, VMEM_SPEC]
    return pl.pallas_call(
        functools.partial(pack_kernel, select is not None),
        out_shape=jax.ShapeDtypeStruct((kb + ns + extra, width), BF),
        in_specs=in_specs,
        out_specs=VMEM_SPEC,
        compiler_params=pltpu.CompilerParams(vmem_limit_bytes=VMEM_LIMIT),
        cost_estimate=pl.CostEstimate(
            flops=0, transcendentals=0, bytes_accessed=2 * 2 * (kb + ns + extra) * width
        ),
        name="pack",
    )(*operands)


def solve_kernel(
    first, blocks, kb, tiles_ref, gath_ref, own_ref, *rest
):
    if first:
        slot_ref, sigma_ref, cross_ref, slots_ref = rest[:4]
        lm, lv, raw, sh, sl, mt, lm_sem, s_sem, lv_sem, levels_ref, out_sem = rest[4:]
    else:
        ancestor_ref, sigma_ref, cross_ref = rest[:3]
        lm, lv, raw, sh, sl, mt, lm_sem, s_sem, lv_sem = rest[3:]
    ns = blocks * TILE
    wide = 2 * TILE
    pairs = blocks // 2
    k = kb // TILE
    leaf_id = lax.axis_index("leaf")
    copies = [pltpu.make_async_copy(gath_ref.at[:, pl.ds(0, kb), :], lm, lm_sem)]
    for b in range(k):
        tile = tiles_ref[leaf_id, b]
        if first:
            source = gath_ref.at[tile, pl.ds(kb + ns, 2 * SENT * TILE), :]
        else:
            source = ancestor_ref.at[tile]
        copies.append(pltpu.make_async_copy(source, raw.at[b], s_sem.at[b]))
    lv_copies = []
    for j in range(pairs):
        lv_copies.append(
            pltpu.make_async_copy(
                gath_ref.at[pl.ds(2 * j, 2), pl.ds(kb + wide * j, ns - wide * j), :],
                lv.at[pl.ds(2 * j, 2), pl.ds(wide * j, ns - wide * j), :],
                lv_sem.at[j],
            )
        )
    for copy in copies + lv_copies:
        copy.start()

    def panel(j):
        return jnp.concatenate([lm[2 * j], lm[2 * j + 1]], axis=1)

    copies[0].wait()
    upper = jnp.zeros((kb, TILE), F32)
    for j in range(pairs):
        upper = upper + dot(panel(j), own_ref[pl.ds(wide * j, wide), :])
    upper_high, upper_low = split(upper)
    for b in range(k):
        copies[1 + b].wait()
        if not first:
            codes = raw[b, pl.ds(SENT * TILE, SCALES), :].astype(jnp.int32).astype(F32)
            code_row = lax.broadcasted_iota(jnp.int32, codes.shape, 0)
        for j in range(SENT):
            if first:
                high = raw[b, pl.ds(j * TILE, TILE), :]
                low = raw[b, pl.ds((SENT + j) * TILE, TILE), :]
            else:
                code = jnp.sum(
                    jnp.where(code_row == tiles_ref[leaf_id, (b + j) % k], codes, 0.0),
                    axis=0,
                    keepdims=True,
                )
                scale = jnp.exp2(code * (1.0 / STEPS)) * (1.0 / TOP)
                levels = raw[b, pl.ds(j * TILE, TILE), :].astype(jnp.int32).astype(F32)
                high, low = split(levels * scale)
            a = (b + j) % k
            sh[pl.ds(a * TILE, TILE), pl.ds(b * TILE, TILE)] = high
            sl[pl.ds(a * TILE, TILE), pl.ds(b * TILE, TILE)] = low
            if j == 1:
                sh[pl.ds(b * TILE, TILE), pl.ds(a * TILE, TILE)] = high.astype(F32).T.astype(BF)
                sl[pl.ds(b * TILE, TILE), pl.ds(a * TILE, TILE)] = low.astype(F32).T.astype(BF)
    both = dot(sh[...], jnp.concatenate([upper_high, upper_low], axis=1))
    cross = -(both[:, :TILE] + both[:, TILE:] + dot(sl[...], upper_high))
    cross_ref[...] = cross
    cross_high, cross_low = split(cross.T)
    stacked = jnp.concatenate([cross_high, cross_low], axis=0)
    for j in range(pairs):
        rows = pl.ds(wide * j, wide)
        part = dot(stacked, panel(j))
        middle = own_ref[rows, :].astype(F32).T - (part[:TILE] + part[TILE:])
        middle_high, middle_low = split(middle)
        mt[pl.ds(0, TILE), rows] = middle_high
        mt[pl.ds(TILE, TILE), rows] = middle_low
    codes = []
    for j in range(pairs):
        lv_copies[j].wait()
        total = jnp.zeros((wide, wide), F32)
        for i in range(j, pairs):
            rows = pl.ds(wide * i, wide)
            total = total + dot(
                mt[:, rows], jnp.concatenate([lv[2 * j, rows, :], lv[2 * j + 1, rows, :]], axis=1)
            )
        block = (total[:TILE] + total[TILE:]).T
        sigma_ref[pl.ds(wide * j, wide), :] = block
        if first:
            for i in range(2):
                levels, code = code_tile(block[i * TILE : (i + 1) * TILE])
                levels_ref[pl.ds(wide * j + i * TILE, TILE), :] = levels.astype(jnp.int16)
                codes.append(code)
    if first:
        row_id = lax.axis_index("row")
        levels_ref[pl.ds(ns, SCALES), :] = (
            jnp.concatenate(codes, axis=0).astype(jnp.int32).astype(jnp.int16)
        )
        out_copies = []
        for p in range(slots_ref.shape[0]):
            starts = [pl.multiple_of(pick * TILE, TILE) for pick in sent_tiles(slot_ref, p, row_id)]
            moves = [(start, j * TILE, TILE) for j, start in enumerate(starts)]
            for j, (start, place, size) in enumerate(moves + [(ns, SENT * TILE, SCALES)]):
                out_copies.append(
                    pltpu.make_async_copy(
                        levels_ref.at[pl.ds(start, size), :],
                        slots_ref.at[p, pl.ds(place, size), :],
                        out_sem.at[p * (SENT + 1) + j],
                    )
                )
        for copy in out_copies:
            copy.start()
        for copy in out_copies:
            copy.wait()


def solve(tiles, gathered, own, kb, slot_tiles=None, ancestor=None):
    first = ancestor is None
    blocks = gathered.shape[0]
    ns, width = own.shape
    k = kb // TILE
    outs = [
        jax.ShapeDtypeStruct((ns, width), F32),
        jax.ShapeDtypeStruct((kb, width), F32),
    ]
    out_specs = [VMEM_SPEC, VMEM_SPEC]
    scratch = [
        pltpu.VMEM((blocks, kb, width), BF),
        pltpu.VMEM((blocks, ns, width), BF),
        pltpu.VMEM((k, 2 * SENT * TILE, width), BF)
        if first
        else pltpu.VMEM((k, SENT * TILE + SCALES, width), jnp.int16),
        pltpu.VMEM((kb, kb), BF),
        pltpu.VMEM((kb, kb), BF),
        pltpu.VMEM((2 * TILE, ns), BF),
        pltpu.SemaphoreType.DMA,
        pltpu.SemaphoreType.DMA((k,)),
        pltpu.SemaphoreType.DMA((blocks // 2,)),
    ]
    operands = [tiles, gathered, own]
    in_specs = [SMEM_SPEC, HBM_SPEC, VMEM_SPEC]
    if first:
        operands.append(slot_tiles)
        in_specs.append(SMEM_SPEC)
        count = slot_tiles.shape[0]
        outs.append(jax.ShapeDtypeStruct((count, SENT * TILE + SCALES, width), jnp.int16))
        out_specs.append(HBM_SPEC)
        scratch.append(pltpu.VMEM((ns + SCALES, width), jnp.int16))
        scratch.append(pltpu.SemaphoreType.DMA((count * (SENT + 1),)))
    else:
        operands.append(ancestor)
        in_specs.append(HBM_SPEC)
    return pl.pallas_call(
        functools.partial(solve_kernel, first, blocks, kb),
        out_shape=outs,
        in_specs=in_specs,
        out_specs=out_specs,
        scratch_shapes=scratch,
        compiler_params=pltpu.CompilerParams(vmem_limit_bytes=SOLVE_LIMIT),
        cost_estimate=pl.CostEstimate(
            flops=4 * ns * ns * width, transcendentals=0, bytes_accessed=14 << 20
        ),
        name="solve_first" if first else "solve_second",
    )(*operands)


def body(
    sigma_root,
    linv_one,
    panel_one,
    tiles_one,
    mask_one,
    linv_two,
    panel_two,
    tiles_two,
    mask_two,
    parent,
):
    leaf_id = lax.axis_index("leaf")
    kb = panel_one.shape[1]
    source = lax.dynamic_index_in_dim(parent, leaf_id, 0, keepdims=False)
    packed_one = pack(mask_one[0], panel_one[0], linv_one[0], tiles_one, sigma_root)
    packed_two = pack(mask_two[0], panel_two[0], linv_two[0])
    gathered_one = lax.all_gather(packed_one, "row", axis=0)
    gathered_one, packed_two = lax.optimization_barrier((gathered_one, packed_two))
    gathered_two = lax.all_gather(packed_two, "row", axis=0)
    sigma_first, cross_first, slots = solve(
        tiles_one, gathered_one, linv_one[0], kb, slot_tiles=tiles_two
    )
    arrived = lax.all_to_all(slots, "leaf", split_axis=0, concat_axis=0, tiled=True)
    chosen = lax.dynamic_index_in_dim(arrived, source, 0, keepdims=False)
    ancestor = lax.all_gather(chosen, "row", axis=0)
    sigma_second, cross_second = solve(
        tiles_two, gathered_two, linv_two[0], kb, ancestor=ancestor
    )
    return (sigma_first[None], cross_first[None], sigma_second[None], cross_second[None])


def solution(mesh):
    return jax.shard_map(
        body,
        mesh=mesh,
        in_specs=(
            P(None, "row"),
            P("leaf", None, "row"),
            P("leaf", None, "row"),
            P(),
            P("leaf", None, "row"),
            P("leaf", None, "row"),
            P("leaf", None, "row"),
            P(),
            P("leaf", None, "row"),
            P(),
        ),
        out_specs=(
            P("leaf", None, "row"),
            P("leaf", None, "row"),
            P("leaf", None, "row"),
            P("leaf", None, "row"),
        ),
        check_vma=False,
    )
```

```python
import functools

import jax
import jax.numpy as jnp
from jax import lax
from jax.experimental import pallas as pl
from jax.experimental.pallas import tpu as pltpu
from jax.sharding import PartitionSpec as P

TILE = 128
BF = jnp.bfloat16
F32 = jnp.float32
I16 = jnp.int16
VMEM_SPEC = pl.BlockSpec(memory_space=pltpu.VMEM)
SMEM_SPEC = pl.BlockSpec(memory_space=pltpu.SMEM)
HBM_SPEC = pl.BlockSpec(memory_space=pltpu.HBM)
VMEM_LIMIT = 40 << 20
SOLVE_LIMIT = 60 << 20
SENT = 3
SCALES = 16
STEPS = 256.0
TOP = 32512.0


def split(x):
    high = x.astype(BF)
    return high, (x - high.astype(F32)).astype(BF)


def code_tile(x):
    peak = jnp.max(jnp.abs(x), axis=0, keepdims=True)
    code = jnp.clip(jnp.ceil(jnp.log2(peak) * STEPS), -110.0 * STEPS, 127.0 * STEPS)
    levels = jnp.round(x * (TOP / jnp.exp2(code * (1.0 / STEPS))))
    return levels.astype(jnp.int32).astype(I16), code


def dot(a, b):
    return jnp.dot(a, b, preferred_element_type=F32)


def sent_tiles(tiles_ref, block, row_id):
    count = tiles_ref.shape[1]
    place = jnp.int32(0)
    for a in range(1, count):
        place = jnp.where(tiles_ref[block, a] == row_id, jnp.int32(a), place)
    picks = []
    for j in range(SENT):
        index = place + j
        picks.append(tiles_ref[block, jnp.where(index >= count, index - count, index)])
    return picks


def code_kernel(tiles_ref, select_ref, out_ref):
    picks = sent_tiles(tiles_ref, lax.axis_index("leaf"), lax.axis_index("row"))
    shape = (SCALES, select_ref.shape[1])
    row = lax.broadcasted_iota(jnp.int32, shape, 0)
    codes = jnp.zeros(shape, F32)
    for j in range(SENT):
        start = pl.multiple_of(picks[j] * TILE, TILE)
        levels, code = code_tile(select_ref[pl.ds(start, TILE), :])
        out_ref[pl.ds(j * TILE, TILE), :] = levels
        codes = jnp.where(row == picks[j], code, codes)
    out_ref[pl.ds(SENT * TILE, SCALES), :] = codes.astype(jnp.int32).astype(I16)


def code(tiles, select):
    return pl.pallas_call(
        code_kernel,
        out_shape=jax.ShapeDtypeStruct((SENT * TILE + SCALES, select.shape[1]), I16),
        in_specs=[SMEM_SPEC, VMEM_SPEC],
        out_specs=VMEM_SPEC,
        compiler_params=pltpu.CompilerParams(vmem_limit_bytes=VMEM_LIMIT),
        cost_estimate=pl.CostEstimate(flops=1 << 20, transcendentals=0, bytes_accessed=1 << 20),
        name="code",
    )(tiles, select)


def pack_kernel(blocks, mask_ref, panel_ref, linv_ref, other_ref, out_ref):
    kb = panel_ref.shape[0]
    ns = linv_ref.shape[0]
    cut = other_ref.shape[0]
    half = blocks // 2
    row_id = lax.axis_index("row")
    for a in range(kb // TILE):
        rows = pl.ds(a * TILE, TILE)
        weight = mask_ref[a, 0].astype(F32)
        out_ref[rows, :] = (panel_ref[rows, :].astype(F32) * weight).astype(BF)

    @pl.when(row_id < half)
    def _():
        out_ref[pl.ds(kb, ns - cut), :] = linv_ref[pl.ds(cut, ns - cut), :]

    @pl.when(row_id >= half)
    def _():
        out_ref[pl.ds(kb, cut), :] = other_ref[...]
        for i in range(half - 1):

            @pl.when(i < blocks - 1 - row_id)
            def _():
                start = pl.multiple_of(lax.min(row_id + i, blocks - 1) * TILE, TILE)
                out_ref[pl.ds(kb + i * TILE, TILE), :] = linv_ref[pl.ds(start, TILE), :]

        out_ref[pl.ds(kb + cut, TILE), :] = linv_ref[pl.ds(ns - TILE, TILE), :]


def turn_kernel(linv_ref, turned_ref):
    for c in range(linv_ref.shape[0] // TILE):
        rows = pl.ds(c * TILE, TILE)
        turned_ref[:, rows] = linv_ref[rows, :].astype(F32).T.astype(BF)


def turn(linv):
    ns, width = linv.shape
    return pl.pallas_call(
        turn_kernel,
        out_shape=jax.ShapeDtypeStruct((width, ns), BF),
        in_specs=[VMEM_SPEC],
        out_specs=VMEM_SPEC,
        compiler_params=pltpu.CompilerParams(vmem_limit_bytes=VMEM_LIMIT),
        cost_estimate=pl.CostEstimate(
            flops=0, transcendentals=0, bytes_accessed=2 * 2 * ns * width
        ),
        name="turn",
    )(linv)


def pack(blocks, mask, panel, linv, other):
    kb, width = panel.shape
    ns = linv.shape[0]
    rows = kb + ns - other.shape[0]
    return pl.pallas_call(
        functools.partial(pack_kernel, blocks),
        out_shape=jax.ShapeDtypeStruct((rows, width), BF),
        in_specs=[SMEM_SPEC, VMEM_SPEC, VMEM_SPEC, VMEM_SPEC],
        out_specs=VMEM_SPEC,
        compiler_params=pltpu.CompilerParams(vmem_limit_bytes=VMEM_LIMIT),
        cost_estimate=pl.CostEstimate(
            flops=0, transcendentals=0, bytes_accessed=2 * 2 * rows * width
        ),
        name="pack",
    )(mask, panel, linv, other)


def column_parts(c, blocks, kb):
    ns = blocks * TILE
    cut = (blocks - 1) * TILE // 2
    if c < blocks // 2:
        return [
            (c, kb, ns - cut, cut),
            (blocks - 1 - c, kb + TILE * c, cut - TILE * c, TILE * c),
        ]
    parts = [(c, kb + cut, TILE, ns - TILE)]
    if c < blocks - 1:
        parts.append((c, kb, TILE * (blocks - 1 - c), TILE * c))
    return parts


def solve_kernel(first, blocks, kb, tiles_ref, gath_ref, own_ref, turned_ref, ancestor_ref, *rest):
    if first:
        slot_ref, sigma_ref, cross_ref, slots_ref = rest[:4]
        lm, lv, raw, sh, sl, mt, lm_sem, s_sem, lv_sem, levels_ref, out_sem = rest[4:]
    else:
        sigma_ref, cross_ref = rest[:2]
        lm, lv, raw, sh, sl, mt, lm_sem, s_sem, lv_sem = rest[2:]
    ns = blocks * TILE
    wide = 2 * TILE
    pairs = blocks // 2
    k = kb // TILE
    leaf_id = lax.axis_index("leaf")
    lm_copies = [
        pltpu.make_async_copy(
            gath_ref.at[c, pl.ds(0, kb), :], lm.at[:, pl.ds(c * TILE, TILE)], lm_sem.at[c]
        )
        for c in range(blocks)
    ]
    s_copies = [
        pltpu.make_async_copy(ancestor_ref.at[tiles_ref[leaf_id, b]], raw.at[b], s_sem.at[b])
        for b in range(k)
    ]
    lv_copies = []
    for c in range(blocks):
        for block, start, size, place in column_parts(c, blocks, kb):
            lv_copies.append(
                pltpu.make_async_copy(
                    gath_ref.at[block, pl.ds(start, size), :],
                    lv.at[pl.ds(place, size), pl.ds(c * TILE, TILE)],
                    lv_sem.at[len(lv_copies)],
                )
            )
    for copy in lm_copies + s_copies + lv_copies:
        copy.start()
    for j in range(pairs):
        lv[pl.ds(wide * j, TILE), pl.ds(wide * j + TILE, TILE)] = jnp.zeros((TILE, TILE), BF)

    for copy in s_copies:
        copy.wait()
    for b in range(k):
        codes = raw[b, pl.ds(SENT * TILE, SCALES), :].astype(jnp.int32).astype(F32)
        code_row = lax.broadcasted_iota(jnp.int32, codes.shape, 0)
        for j in range(SENT):
            a = (b + j) % k
            code = jnp.sum(
                jnp.where(code_row == tiles_ref[leaf_id, a], codes, 0.0), axis=0, keepdims=True
            )
            scale = jnp.exp2(code * (1.0 / STEPS)) * (1.0 / TOP)
            values = raw[b, pl.ds(j * TILE, TILE), :].astype(jnp.int32).astype(F32) * scale
            high, low = split(values)
            sh[pl.ds(a * TILE, TILE), pl.ds(b * TILE, TILE)] = high
            sl[pl.ds(a * TILE, TILE), pl.ds(b * TILE, TILE)] = low
            if j == 1:
                high, low = split(values.T)
                sh[pl.ds(b * TILE, TILE), pl.ds(a * TILE, TILE)] = high
                sl[pl.ds(b * TILE, TILE), pl.ds(a * TILE, TILE)] = low
    for copy in lm_copies:
        copy.wait()
    upper_high, upper_low = split(dot(lm[...], own_ref[...]))
    both = dot(sh[...], jnp.concatenate([upper_high, upper_low], axis=1))
    cross = -(both[:, :TILE] + both[:, TILE:] + dot(sl[...], upper_high))
    cross_ref[...] = cross
    cross_high, cross_low = split(cross.T)
    stacked = jnp.concatenate([cross_high, cross_low], axis=0)
    for j in range(pairs):
        rows = pl.ds(wide * j, wide)
        part = dot(stacked, lm[:, rows])
        middle = turned_ref[:, rows].astype(F32) - (part[:TILE] + part[TILE:])
        middle_high, middle_low = split(middle)
        mt[pl.ds(0, TILE), rows] = middle_high
        mt[pl.ds(TILE, TILE), rows] = middle_low
    for copy in lv_copies:
        copy.wait()
    codes = []
    for j in range(pairs):
        rest_rows = pl.ds(wide * j, ns - wide * j)
        total = dot(mt[:, rest_rows], lv[rest_rows, pl.ds(wide * j, wide)])
        block = (total[:TILE] + total[TILE:]).T
        sigma_ref[pl.ds(wide * j, wide), :] = block
        if first:
            for i in range(2):
                levels, code = code_tile(block[i * TILE : (i + 1) * TILE])
                levels_ref[pl.ds(wide * j + i * TILE, TILE), :] = levels
                codes.append(code)
    if first:
        row_id = lax.axis_index("row")
        levels_ref[pl.ds(ns, SCALES), :] = (
            jnp.concatenate(codes, axis=0).astype(jnp.int32).astype(I16)
        )
        out_copies = []
        for p in range(slots_ref.shape[0]):
            starts = [pl.multiple_of(pick * TILE, TILE) for pick in sent_tiles(slot_ref, p, row_id)]
            moves = [(start, j * TILE, TILE) for j, start in enumerate(starts)]
            for j, (start, place, size) in enumerate(moves + [(ns, SENT * TILE, SCALES)]):
                out_copies.append(
                    pltpu.make_async_copy(
                        levels_ref.at[pl.ds(start, size), :],
                        slots_ref.at[p, pl.ds(place, size), :],
                        out_sem.at[p * (SENT + 1) + j],
                    )
                )
        for copy in out_copies:
            copy.start()
        for copy in out_copies:
            copy.wait()


def solve(tiles, gathered, own, turned, kb, ancestor, slot_tiles=None):
    first = slot_tiles is not None
    blocks = gathered.shape[0]
    ns, width = own.shape
    k = kb // TILE
    outs = [
        jax.ShapeDtypeStruct((ns, width), F32),
        jax.ShapeDtypeStruct((kb, width), F32),
    ]
    out_specs = [VMEM_SPEC, VMEM_SPEC]
    parts = sum(len(column_parts(c, blocks, kb)) for c in range(blocks))
    scratch = [
        pltpu.VMEM((kb, ns), BF),
        pltpu.VMEM((ns, ns), BF),
        pltpu.VMEM((k,) + ancestor.shape[1:], I16),
        pltpu.VMEM((kb, kb), BF),
        pltpu.VMEM((kb, kb), BF),
        pltpu.VMEM((2 * TILE, ns), BF),
        pltpu.SemaphoreType.DMA((blocks,)),
        pltpu.SemaphoreType.DMA((k,)),
        pltpu.SemaphoreType.DMA((parts,)),
    ]
    operands = [tiles, gathered, own, turned, ancestor]
    in_specs = [SMEM_SPEC, HBM_SPEC, VMEM_SPEC, VMEM_SPEC, HBM_SPEC]
    if first:
        operands.append(slot_tiles)
        in_specs.append(SMEM_SPEC)
        count = slot_tiles.shape[0]
        outs.append(jax.ShapeDtypeStruct((count, SENT * TILE + SCALES, width), I16))
        out_specs.append(HBM_SPEC)
        scratch.append(pltpu.VMEM((ns + SCALES, width), I16))
        scratch.append(pltpu.SemaphoreType.DMA((count * (SENT + 1),)))
    return pl.pallas_call(
        functools.partial(solve_kernel, first, blocks, kb),
        out_shape=outs,
        in_specs=in_specs,
        out_specs=out_specs,
        scratch_shapes=scratch,
        compiler_params=pltpu.CompilerParams(vmem_limit_bytes=SOLVE_LIMIT),
        cost_estimate=pl.CostEstimate(
            flops=4 * ns * ns * width, transcendentals=0, bytes_accessed=14 << 20
        ),
        name="solve_first" if first else "solve_second",
    )(*operands)


def body(
    sigma_root,
    linv_one,
    panel_one,
    tiles_one,
    mask_one,
    linv_two,
    panel_two,
    tiles_two,
    mask_two,
    parent,
):
    leaf_id = lax.axis_index("leaf")
    kb = panel_one.shape[1]
    ns, width = linv_one.shape[1:]
    blocks = ns // TILE
    cut = (blocks - 1) * TILE // 2
    fold = [(i, blocks - 1 - i) for i in range(blocks // 2)]
    source = lax.dynamic_index_in_dim(parent, leaf_id, 0, keepdims=False)

    other_one = lax.ppermute(linv_one[0, :cut], "row", fold)
    coded_one = code(tiles_one, sigma_root)
    turned_one = turn(linv_one[0])
    packed_one = pack(blocks, mask_one[0], panel_one[0], linv_one[0], other_one)
    packed_one, coded_one, turned_one = lax.optimization_barrier(
        (packed_one, coded_one, turned_one)
    )
    gathered_one = lax.all_gather(packed_one, "row", axis=0)
    ancestor_one = lax.all_gather(coded_one, "row", axis=0)
    ancestor_one, later_two = lax.optimization_barrier((ancestor_one, linv_two[0]))
    other_two = lax.ppermute(later_two[:cut], "row", fold)
    turned_two = turn(later_two)
    packed_two = pack(blocks, mask_two[0], panel_two[0], later_two, other_two)
    gathered_one, packed_two = lax.optimization_barrier((gathered_one, packed_two))
    gathered_two = lax.all_gather(packed_two, "row", axis=0)
    sigma_first, cross_first, slots = solve(
        tiles_one, gathered_one, linv_one[0], turned_one, kb, ancestor_one, tiles_two
    )
    arrived = lax.all_to_all(slots, "leaf", split_axis=0, concat_axis=0, tiled=True)
    chosen = lax.dynamic_index_in_dim(arrived, source, 0, keepdims=False)
    ancestor_two = lax.all_gather(chosen, "row", axis=0)
    sigma_second, cross_second = solve(
        tiles_two, gathered_two, linv_two[0], turned_two, kb, ancestor_two
    )
    return (sigma_first[None], cross_first[None], sigma_second[None], cross_second[None])


def solution(mesh):
    return jax.shard_map(
        body,
        mesh=mesh,
        in_specs=(
            P(None, "row"),
            P("leaf", None, "row"),
            P("leaf", None, "row"),
            P(),
            P("leaf", None, "row"),
            P("leaf", None, "row"),
            P("leaf", None, "row"),
            P(),
            P("leaf", None, "row"),
            P(),
        ),
        out_specs=(
            P("leaf", None, "row"),
            P("leaf", None, "row"),
            P("leaf", None, "row"),
            P("leaf", None, "row"),
        ),
        check_vma=False,
    )
```

```python
import functools

import jax
import jax.numpy as jnp
from jax import lax
from jax.experimental import pallas as pl
from jax.experimental.pallas import tpu as pltpu
from jax.sharding import PartitionSpec as P

TILE = 128
BF = jnp.bfloat16
F32 = jnp.float32
I16 = jnp.int16
VMEM_SPEC = pl.BlockSpec(memory_space=pltpu.VMEM)
SMEM_SPEC = pl.BlockSpec(memory_space=pltpu.SMEM)
HBM_SPEC = pl.BlockSpec(memory_space=pltpu.HBM)
VMEM_LIMIT = 40 << 20
SOLVE_LIMIT = 60 << 20
SENT = 3
SCALES = 16
STEPS = 256.0
TOP = 32512.0


def split(x):
    high = x.astype(BF)
    return high, (x - high.astype(F32)).astype(BF)


def code_tile(x):
    peak = jnp.max(jnp.abs(x), axis=0, keepdims=True)
    code = jnp.clip(jnp.ceil(jnp.log2(peak) * STEPS), -110.0 * STEPS, 127.0 * STEPS)
    levels = jnp.round(x * (TOP / jnp.exp2(code * (1.0 / STEPS))))
    return levels.astype(jnp.int32).astype(I16), code


def dot(a, b):
    return jnp.dot(a, b, preferred_element_type=F32)


def sent_tiles(tiles_ref, block, row_id):
    count = tiles_ref.shape[1]
    place = jnp.int32(0)
    for a in range(1, count):
        place = jnp.where(tiles_ref[block, a] == row_id, jnp.int32(a), place)
    picks = []
    for j in range(SENT):
        index = place + j
        picks.append(tiles_ref[block, jnp.where(index >= count, index - count, index)])
    return picks


def code_kernel(tiles_ref, select_ref, out_ref):
    picks = sent_tiles(tiles_ref, lax.axis_index("leaf"), lax.axis_index("row"))
    shape = (SCALES, select_ref.shape[1])
    row = lax.broadcasted_iota(jnp.int32, shape, 0)
    codes = jnp.zeros(shape, F32)
    for j in range(SENT):
        start = pl.multiple_of(picks[j] * TILE, TILE)
        levels, code = code_tile(select_ref[pl.ds(start, TILE), :])
        out_ref[pl.ds(j * TILE, TILE), :] = levels
        codes = jnp.where(row == picks[j], code, codes)
    out_ref[pl.ds(SENT * TILE, SCALES), :] = codes.astype(jnp.int32).astype(I16)


def code(tiles, select):
    return pl.pallas_call(
        code_kernel,
        out_shape=jax.ShapeDtypeStruct((SENT * TILE + SCALES, select.shape[1]), I16),
        in_specs=[SMEM_SPEC, VMEM_SPEC],
        out_specs=VMEM_SPEC,
        compiler_params=pltpu.CompilerParams(vmem_limit_bytes=VMEM_LIMIT),
        cost_estimate=pl.CostEstimate(flops=1 << 20, transcendentals=0, bytes_accessed=1 << 20),
        name="code",
    )(tiles, select)


def pack_kernel(blocks, mask_ref, panel_ref, linv_ref, other_ref, out_ref):
    kb = panel_ref.shape[0]
    ns = linv_ref.shape[0]
    cut = other_ref.shape[0]
    half = blocks // 2
    row_id = lax.axis_index("row")
    for a in range(kb // TILE):
        rows = pl.ds(a * TILE, TILE)
        weight = mask_ref[a, 0].astype(F32)
        out_ref[rows, :] = (panel_ref[rows, :].astype(F32) * weight).astype(BF)

    @pl.when(row_id < half)
    def _():
        out_ref[pl.ds(kb, ns - cut), :] = linv_ref[pl.ds(cut, ns - cut), :]

    @pl.when(row_id >= half)
    def _():
        out_ref[pl.ds(kb, cut), :] = other_ref[...]
        for i in range(half - 1):

            @pl.when(i < blocks - 1 - row_id)
            def _():
                start = pl.multiple_of(lax.min(row_id + i, blocks - 1) * TILE, TILE)
                out_ref[pl.ds(kb + i * TILE, TILE), :] = linv_ref[pl.ds(start, TILE), :]

        out_ref[pl.ds(kb + cut, TILE), :] = linv_ref[pl.ds(ns - TILE, TILE), :]


def turn_kernel(linv_ref, turned_ref):
    for c in range(linv_ref.shape[0] // TILE):
        rows = pl.ds(c * TILE, TILE)
        turned_ref[:, rows] = linv_ref[rows, :].astype(F32).T.astype(BF)


def turn(linv):
    ns, width = linv.shape
    return pl.pallas_call(
        turn_kernel,
        out_shape=jax.ShapeDtypeStruct((width, ns), BF),
        in_specs=[VMEM_SPEC],
        out_specs=VMEM_SPEC,
        compiler_params=pltpu.CompilerParams(vmem_limit_bytes=VMEM_LIMIT),
        cost_estimate=pl.CostEstimate(
            flops=0, transcendentals=0, bytes_accessed=2 * 2 * ns * width
        ),
        name="turn",
    )(linv)


def pack(blocks, mask, panel, linv, other):
    kb, width = panel.shape
    ns = linv.shape[0]
    rows = kb + ns - other.shape[0]
    return pl.pallas_call(
        functools.partial(pack_kernel, blocks),
        out_shape=jax.ShapeDtypeStruct((rows, width), BF),
        in_specs=[SMEM_SPEC, VMEM_SPEC, VMEM_SPEC, VMEM_SPEC],
        out_specs=VMEM_SPEC,
        compiler_params=pltpu.CompilerParams(vmem_limit_bytes=VMEM_LIMIT),
        cost_estimate=pl.CostEstimate(
            flops=0, transcendentals=0, bytes_accessed=2 * 2 * rows * width
        ),
        name="pack",
    )(mask, panel, linv, other)


def column_parts(c, blocks, kb):
    ns = blocks * TILE
    cut = (blocks - 1) * TILE // 2
    if c < blocks // 2:
        return [
            (c, kb, ns - cut, cut),
            (blocks - 1 - c, kb + TILE * c, cut - TILE * c, TILE * c),
        ]
    parts = [(c, kb + cut, TILE, ns - TILE)]
    if c < blocks - 1:
        parts.append((c, kb, TILE * (blocks - 1 - c), TILE * c))
    return parts


def solve_kernel(first, blocks, kb, tiles_ref, gath_ref, own_ref, turned_ref, ancestor_ref, *rest):
    if first:
        slot_ref, sigma_ref, cross_ref, slots_ref = rest[:4]
        rest = rest[4:]
        levels_ref, picks_ref, out_sem = rest[-3:]
    else:
        sigma_ref, cross_ref = rest[:2]
        rest = rest[2:]
    lm, lv, own, turned, raw, sh, sl, mt, sg, cr, lm_sem, s_sem, lv_sem, own_sem, res_sem = rest[:15]
    ns = blocks * TILE
    wide = 2 * TILE
    pairs = blocks // 2
    k = kb // TILE
    leaf_id = lax.axis_index("leaf")
    s_copies = [
        pltpu.make_async_copy(ancestor_ref.at[tiles_ref[leaf_id, b]], raw.at[b], s_sem.at[b])
        for b in range(k)
    ]
    own_copy = pltpu.make_async_copy(own_ref, own, own_sem.at[0])
    turned_copy = pltpu.make_async_copy(turned_ref, turned, own_sem.at[1])
    lm_copies = [
        pltpu.make_async_copy(
            gath_ref.at[c, pl.ds(0, kb), :], lm.at[:, pl.ds(c * TILE, TILE)], lm_sem.at[c]
        )
        for c in range(blocks)
    ]
    lv_copies = []
    for c in range(blocks):
        for block, start, size, place in column_parts(c, blocks, kb):
            lv_copies.append(
                pltpu.make_async_copy(
                    gath_ref.at[block, pl.ds(start, size), :],
                    lv.at[pl.ds(place, size), pl.ds(c * TILE, TILE)],
                    lv_sem.at[len(lv_copies)],
                )
            )
    for copy in s_copies + [own_copy] + lm_copies + [turned_copy] + lv_copies:
        copy.start()
    for j in range(pairs):
        lv[pl.ds(wide * j, TILE), pl.ds(wide * j + TILE, TILE)] = jnp.zeros((TILE, TILE), BF)
    if first:
        row_id = lax.axis_index("row")
        for p in range(slots_ref.shape[0]):
            for j, pick in enumerate(sent_tiles(slot_ref, p, row_id)):
                picks_ref[p * SENT + j] = pick

    for copy in s_copies:
        copy.wait()
    for b in range(k):
        codes = raw[b, pl.ds(SENT * TILE, SCALES), :].astype(jnp.int32).astype(F32)
        code_row = lax.broadcasted_iota(jnp.int32, codes.shape, 0)
        for j in range(SENT):
            a = (b + j) % k
            code = jnp.sum(
                jnp.where(code_row == tiles_ref[leaf_id, a], codes, 0.0), axis=0, keepdims=True
            )
            scale = jnp.exp2(code * (1.0 / STEPS)) * (1.0 / TOP)
            values = raw[b, pl.ds(j * TILE, TILE), :].astype(jnp.int32).astype(F32) * scale
            high, low = split(values)
            sh[pl.ds(a * TILE, TILE), pl.ds(b * TILE, TILE)] = high
            sl[pl.ds(a * TILE, TILE), pl.ds(b * TILE, TILE)] = low
            if j == 1:
                high, low = split(values.T)
                sh[pl.ds(b * TILE, TILE), pl.ds(a * TILE, TILE)] = high
                sl[pl.ds(b * TILE, TILE), pl.ds(a * TILE, TILE)] = low
    own_copy.wait()
    for copy in lm_copies:
        copy.wait()
    upper = jnp.concatenate(
        [dot(lm[pl.ds(i * (kb // 2), kb // 2), :], own[...]) for i in range(2)], axis=0
    )
    upper_high, upper_low = split(upper)
    upper_both = jnp.concatenate([upper_high, upper_low], axis=1)
    crosses = []
    for i in range(2):
        rows = pl.ds(i * (kb // 2), kb // 2)
        both = dot(sh[rows, :], upper_both)
        crosses.append(-(both[:, :TILE] + both[:, TILE:] + dot(sl[rows, :], upper_high)))
    cross = jnp.concatenate(crosses, axis=0)
    cr[...] = cross
    cross_copy = pltpu.make_async_copy(cr, cross_ref, own_sem.at[0])
    cross_copy.start()
    cross_high, cross_low = split(cross.T)
    stacked = jnp.concatenate([cross_high, cross_low], axis=0)
    turned_copy.wait()
    for copy in lv_copies:
        copy.wait()
    for j in range(pairs):
        rows = pl.ds(wide * j, wide)
        part = dot(stacked, lm[:, rows])
        middle = turned[:, rows].astype(F32) - (part[:TILE] + part[TILE:])
        middle_high, middle_low = split(middle)
        mt[pl.ds(0, TILE), rows] = middle_high
        mt[pl.ds(TILE, TILE), rows] = middle_low
    codes = []
    out_copies = []
    for j in range(pairs):
        rows = pl.ds(wide * j, wide)
        rest_rows = pl.ds(wide * j, ns - wide * j)
        total = dot(mt[:, rest_rows], lv[rest_rows, rows])
        block = (total[:TILE] + total[TILE:]).T
        sg[rows, :] = block
        if first:
            for i in range(2):
                levels, code = code_tile(block[i * TILE : (i + 1) * TILE])
                levels_ref[pl.ds(wide * j + i * TILE, TILE), :] = levels
                codes.append(code)
        else:
            copy = pltpu.make_async_copy(sg.at[rows], sigma_ref.at[rows], res_sem.at[j])
            copy.start()
            out_copies.append(copy)
    if first:
        levels_ref[pl.ds(ns, SCALES), :] = (
            jnp.concatenate(codes, axis=0).astype(jnp.int32).astype(I16)
        )
        for p in range(slots_ref.shape[0]):
            starts = [
                pl.multiple_of(picks_ref[p * SENT + j] * TILE, TILE) for j in range(SENT)
            ]
            moves = [(start, j * TILE, TILE) for j, start in enumerate(starts)]
            for j, (start, place, size) in enumerate(moves + [(ns, SENT * TILE, SCALES)]):
                copy = pltpu.make_async_copy(
                    levels_ref.at[pl.ds(start, size), :],
                    slots_ref.at[p, pl.ds(place, size), :],
                    out_sem.at[p * (SENT + 1) + j],
                )
                copy.start()
                out_copies.append(copy)
        copy = pltpu.make_async_copy(sg, sigma_ref, res_sem.at[0])
        copy.start()
        out_copies.append(copy)
    cross_copy.wait()
    for copy in out_copies:
        copy.wait()


def solve(tiles, gathered, own, turned, kb, ancestor, slot_tiles=None):
    first = slot_tiles is not None
    blocks = gathered.shape[0]
    ns, width = own.shape
    k = kb // TILE
    outs = [
        jax.ShapeDtypeStruct((ns, width), F32),
        jax.ShapeDtypeStruct((kb, width), F32),
    ]
    parts = sum(len(column_parts(c, blocks, kb)) for c in range(blocks))
    scratch = [
        pltpu.VMEM((kb, ns), BF),
        pltpu.VMEM((ns, ns), BF),
        pltpu.VMEM((ns, width), BF),
        pltpu.VMEM((width, ns), BF),
        pltpu.VMEM((k,) + ancestor.shape[1:], I16),
        pltpu.VMEM((kb, kb), BF),
        pltpu.VMEM((kb, kb), BF),
        pltpu.VMEM((2 * TILE, ns), BF),
        pltpu.VMEM((ns, width), F32),
        pltpu.VMEM((kb, width), F32),
        pltpu.SemaphoreType.DMA((blocks,)),
        pltpu.SemaphoreType.DMA((k,)),
        pltpu.SemaphoreType.DMA((parts,)),
        pltpu.SemaphoreType.DMA((2,)),
        pltpu.SemaphoreType.DMA((blocks // 2,)),
    ]
    operands = [tiles, gathered, own, turned, ancestor]
    in_specs = [SMEM_SPEC, HBM_SPEC, HBM_SPEC, HBM_SPEC, HBM_SPEC]
    if first:
        operands.append(slot_tiles)
        in_specs.append(SMEM_SPEC)
        count = slot_tiles.shape[0]
        outs.append(jax.ShapeDtypeStruct((count, SENT * TILE + SCALES, width), I16))
        scratch.append(pltpu.VMEM((ns + SCALES, width), I16))
        scratch.append(pltpu.SMEM((count * SENT,), jnp.int32))
        scratch.append(pltpu.SemaphoreType.DMA((count * (SENT + 1),)))
    return pl.pallas_call(
        functools.partial(solve_kernel, first, blocks, kb),
        out_shape=outs,
        in_specs=in_specs,
        out_specs=[HBM_SPEC] * len(outs),
        scratch_shapes=scratch,
        compiler_params=pltpu.CompilerParams(vmem_limit_bytes=SOLVE_LIMIT),
        cost_estimate=pl.CostEstimate(
            flops=4 * ns * ns * width, transcendentals=0, bytes_accessed=14 << 20
        ),
        name="solve_first" if first else "solve_second",
    )(*operands)


def body(
    sigma_root,
    linv_one,
    panel_one,
    tiles_one,
    mask_one,
    linv_two,
    panel_two,
    tiles_two,
    mask_two,
    parent,
):
    leaf_id = lax.axis_index("leaf")
    kb = panel_one.shape[1]
    ns, width = linv_one.shape[1:]
    blocks = ns // TILE
    cut = (blocks - 1) * TILE // 2
    fold = [(i, blocks - 1 - i) for i in range(blocks // 2)]
    source = lax.dynamic_index_in_dim(parent, leaf_id, 0, keepdims=False)

    other_one = lax.ppermute(linv_one[0, :cut], "row", fold)
    coded_one = code(tiles_one, sigma_root)
    turned_one = turn(linv_one[0])
    other_one, later_two = lax.optimization_barrier((other_one, linv_two[0]))
    packed_one = pack(blocks, mask_one[0], panel_one[0], linv_one[0], other_one)
    packed_one, coded_one, turned_one = lax.optimization_barrier(
        (packed_one, coded_one, turned_one)
    )
    gathered_one = lax.all_gather(packed_one, "row", axis=0)
    other_two = lax.ppermute(later_two[:cut], "row", fold)
    ancestor_one = lax.all_gather(coded_one, "row", axis=0)
    ancestor_one, other_two = lax.optimization_barrier((ancestor_one, other_two))
    turned_two = turn(later_two)
    packed_two = pack(blocks, mask_two[0], panel_two[0], later_two, other_two)
    gathered_one, packed_two = lax.optimization_barrier((gathered_one, packed_two))
    gathered_two = lax.all_gather(packed_two, "row", axis=0)
    sigma_first, cross_first, slots = solve(
        tiles_one, gathered_one, linv_one[0], turned_one, kb, ancestor_one, tiles_two
    )
    arrived = lax.all_to_all(slots, "leaf", split_axis=0, concat_axis=0, tiled=True)
    chosen = lax.dynamic_index_in_dim(arrived, source, 0, keepdims=False)
    ancestor_two = lax.all_gather(chosen, "row", axis=0)
    sigma_second, cross_second = solve(
        tiles_two, gathered_two, linv_two[0], turned_two, kb, ancestor_two
    )
    return (sigma_first[None], cross_first[None], sigma_second[None], cross_second[None])


def solution(mesh):
    return jax.shard_map(
        body,
        mesh=mesh,
        in_specs=(
            P(None, "row"),
            P("leaf", None, "row"),
            P("leaf", None, "row"),
            P(),
            P("leaf", None, "row"),
            P("leaf", None, "row"),
            P("leaf", None, "row"),
            P(),
            P("leaf", None, "row"),
            P(),
        ),
        out_specs=(
            P("leaf", None, "row"),
            P("leaf", None, "row"),
            P("leaf", None, "row"),
            P("leaf", None, "row"),
        ),
        check_vma=False,
    )
```

```python
import functools

import jax
import jax.numpy as jnp
from jax import lax
from jax.experimental import pallas as pl
from jax.experimental.pallas import tpu as pltpu
from jax.sharding import PartitionSpec as P

TILE = 128
BF = jnp.bfloat16
F32 = jnp.float32
I16 = jnp.int16
VMEM_SPEC = pl.BlockSpec(memory_space=pltpu.VMEM)
SMEM_SPEC = pl.BlockSpec(memory_space=pltpu.SMEM)
HBM_SPEC = pl.BlockSpec(memory_space=pltpu.HBM)
VMEM_LIMIT = 40 << 20
SOLVE_LIMIT = 60 << 20
SENT = 3
HALF = TILE // 2
PIECES = (TILE, TILE, HALF)
DATA = sum(PIECES)
SCALES = 16
STEPS = 256.0
TOP = 32512.0


def split(x):
    high = x.astype(BF)
    return high, (x - high.astype(F32)).astype(BF)


def code_tile(x):
    peak = jnp.max(jnp.abs(x), axis=0, keepdims=True)
    code = jnp.clip(jnp.ceil(jnp.log2(peak) * STEPS), -110.0 * STEPS, 127.0 * STEPS)
    levels = jnp.round(x * (TOP / jnp.exp2(code * (1.0 / STEPS))))
    return levels.astype(jnp.int32), code


def right_half(x):
    lane = lax.broadcasted_iota(jnp.int32, (HALF, TILE), 1)
    return jnp.where(lane < HALF, pltpu.roll(x[:HALF], HALF, 1), x[HALF:])


def dot(a, b):
    return jnp.dot(a, b, preferred_element_type=F32)


def sent_tiles(tiles_ref, block, row_id):
    count = tiles_ref.shape[0]
    place = jnp.int32(0)
    for a in range(1, count):
        place = jnp.where(tiles_ref[a, block] == row_id, jnp.int32(a), place)
    picks = []
    for j in range(SENT):
        index = place + j
        picks.append(tiles_ref[jnp.where(index >= count, index - count, index), block])
    return picks, place < count // 2


def code_kernel(tiles_ref, select_ref, out_ref):
    picks, early = sent_tiles(tiles_ref, lax.axis_index("leaf"), lax.axis_index("row"))
    shape = (SCALES, select_ref.shape[1])
    row = lax.broadcasted_iota(jnp.int32, shape, 0)
    codes = jnp.zeros(shape, F32)
    for j in range(SENT):
        start = pl.multiple_of(picks[j] * TILE, TILE)
        levels, code = code_tile(select_ref[pl.ds(start, TILE), :])
        if PIECES[j] == HALF:
            levels = jnp.where(early, right_half(levels), levels[:HALF])
        out_ref[pl.ds(j * TILE, PIECES[j]), :] = levels.astype(I16)
        codes = jnp.where(row == picks[j], code, codes)
    out_ref[pl.ds(DATA, SCALES), :] = codes.astype(jnp.int32).astype(I16)


def code(tiles, select):
    return pl.pallas_call(
        code_kernel,
        out_shape=jax.ShapeDtypeStruct((DATA + SCALES, select.shape[1]), I16),
        in_specs=[SMEM_SPEC, VMEM_SPEC],
        out_specs=VMEM_SPEC,
        compiler_params=pltpu.CompilerParams(vmem_limit_bytes=VMEM_LIMIT),
        cost_estimate=pl.CostEstimate(flops=1 << 20, transcendentals=0, bytes_accessed=1 << 20),
        name="code",
    )(tiles, select)


def pack_kernel(blocks, mask_ref, panel_ref, linv_ref, other_ref, out_ref):
    kb = panel_ref.shape[0]
    ns = linv_ref.shape[0]
    cut = other_ref.shape[0]
    half = blocks // 2
    row_id = lax.axis_index("row")
    for a in range(kb // TILE):
        rows = pl.ds(a * TILE, TILE)
        weight = mask_ref[a].astype(F32)
        out_ref[rows, :] = (panel_ref[rows, :].astype(F32) * weight).astype(BF)

    @pl.when(row_id < half)
    def _():
        out_ref[pl.ds(kb, ns - cut), :] = linv_ref[pl.ds(cut, ns - cut), :]

    @pl.when(row_id >= half)
    def _():
        out_ref[pl.ds(kb, cut), :] = other_ref[...]
        for i in range(half - 1):

            @pl.when(i < blocks - 1 - row_id)
            def _():
                start = pl.multiple_of(lax.min(row_id + i, blocks - 1) * TILE, TILE)
                out_ref[pl.ds(kb + i * TILE, TILE), :] = linv_ref[pl.ds(start, TILE), :]

        out_ref[pl.ds(kb + cut, TILE), :] = linv_ref[pl.ds(ns - TILE, TILE), :]


def turn_kernel(linv_ref, turned_ref):
    for c in range(linv_ref.shape[0] // TILE):
        rows = pl.ds(c * TILE, TILE)
        turned_ref[:, rows] = linv_ref[rows, :].astype(F32).T.astype(BF)


def turn(linv):
    ns, width = linv.shape
    return pl.pallas_call(
        turn_kernel,
        out_shape=jax.ShapeDtypeStruct((width, ns), BF),
        in_specs=[VMEM_SPEC],
        out_specs=VMEM_SPEC,
        compiler_params=pltpu.CompilerParams(vmem_limit_bytes=VMEM_LIMIT),
        cost_estimate=pl.CostEstimate(
            flops=0, transcendentals=0, bytes_accessed=2 * 2 * ns * width
        ),
        name="turn",
    )(linv)


def pack(blocks, mask, panel, linv, other):
    kb, width = panel.shape
    ns = linv.shape[0]
    rows = kb + ns - other.shape[0]
    return pl.pallas_call(
        functools.partial(pack_kernel, blocks),
        out_shape=jax.ShapeDtypeStruct((rows, width), BF),
        in_specs=[SMEM_SPEC, VMEM_SPEC, VMEM_SPEC, VMEM_SPEC],
        out_specs=VMEM_SPEC,
        compiler_params=pltpu.CompilerParams(vmem_limit_bytes=VMEM_LIMIT),
        cost_estimate=pl.CostEstimate(
            flops=0, transcendentals=0, bytes_accessed=2 * 2 * rows * width
        ),
        name="pack",
    )(mask, panel, linv, other)


def column_parts(c, blocks, kb):
    ns = blocks * TILE
    cut = (blocks - 1) * TILE // 2
    if c < blocks // 2:
        return [
            (c, kb, ns - cut, cut),
            (blocks - 1 - c, kb + TILE * c, cut - TILE * c, TILE * c),
        ]
    parts = [(c, kb + cut, TILE, ns - TILE)]
    if c < blocks - 1:
        parts.append((c, kb, TILE * (blocks - 1 - c), TILE * c))
    return parts


def solve_kernel(first, blocks, kb, tiles_ref, gath_ref, own_ref, turned_ref, ancestor_ref, *rest):
    if first:
        slot_ref, sigma_ref, cross_ref, slots_ref = rest[:4]
        rest = rest[4:]
        levels_ref, picks_ref, out_sem = rest[-3:]
    else:
        sigma_ref, cross_ref = rest[:2]
        rest = rest[2:]
    lm, lv, own, turned, raw, sh, sl, mt, sg, cr, lm_sem, s_sem, lv_sem, own_sem, res_sem = rest[:15]
    ns = blocks * TILE
    wide = 2 * TILE
    pairs = blocks // 2
    k = kb // TILE
    leaf_id = lax.axis_index("leaf")
    s_copies = [
        pltpu.make_async_copy(ancestor_ref.at[tiles_ref[b, leaf_id]], raw.at[b], s_sem.at[b])
        for b in range(k)
    ]
    own_copy = pltpu.make_async_copy(own_ref, own, own_sem.at[0])
    turned_copy = pltpu.make_async_copy(turned_ref, turned, own_sem.at[1])
    lm_copies = [
        pltpu.make_async_copy(
            gath_ref.at[c, pl.ds(0, kb), :], lm.at[:, pl.ds(c * TILE, TILE)], lm_sem.at[c]
        )
        for c in range(blocks)
    ]
    lv_copies = []
    for c in range(blocks):
        for block, start, size, place in column_parts(c, blocks, kb):
            lv_copies.append(
                pltpu.make_async_copy(
                    gath_ref.at[block, pl.ds(start, size), :],
                    lv.at[pl.ds(place, size), pl.ds(c * TILE, TILE)],
                    lv_sem.at[len(lv_copies)],
                )
            )
    for copy in s_copies + [own_copy] + lm_copies + [turned_copy] + lv_copies:
        copy.start()
    for j in range(pairs):
        lv[pl.ds(wide * j, TILE), pl.ds(wide * j + TILE, TILE)] = jnp.zeros((TILE, TILE), BF)
    if first:
        row_id = lax.axis_index("row")
        for p in range(slots_ref.shape[0]):
            picks, early = sent_tiles(slot_ref, p, row_id)
            for j, pick in enumerate(picks):
                start = pick * TILE
                if PIECES[j] == HALF:
                    start = jnp.where(early, ns + SCALES + pick * HALF, start)
                picks_ref[p * SENT + j] = start

    def store(a, b, values):
        high, low = split(values)
        sh[pl.ds(a * TILE, TILE), pl.ds(b * TILE, TILE)] = high
        sl[pl.ds(a * TILE, TILE), pl.ds(b * TILE, TILE)] = low

    for copy in s_copies:
        copy.wait()
    halves = []
    for b in range(k):
        codes = raw[b, pl.ds(DATA, SCALES), :].astype(jnp.int32).astype(F32)
        code_row = lax.broadcasted_iota(jnp.int32, codes.shape, 0)
        for j in range(SENT):
            a = (b + j) % k
            code = jnp.sum(
                jnp.where(code_row == tiles_ref[a, leaf_id], codes, 0.0), axis=0, keepdims=True
            )
            scale = jnp.exp2(code * (1.0 / STEPS)) * (1.0 / TOP)
            values = raw[b, pl.ds(j * TILE, PIECES[j]), :].astype(jnp.int32).astype(F32)
            if j == 2:
                if b < k // 2:
                    values = jnp.concatenate([pltpu.roll(values, HALF, 1), values], axis=0)
                halves.append(values * scale)
                continue
            values = values * scale
            store(a, b, values)
            if j == 1:
                store(b, a, values.T)
    for b in range(k // 2):
        a = b + k // 2
        values = jnp.concatenate([halves[a], halves[b].T[HALF:]], axis=0)
        store(b, a, values)
        store(a, b, values.T)
    own_copy.wait()
    for copy in lm_copies:
        copy.wait()
    upper = jnp.concatenate(
        [dot(lm[pl.ds(i * (kb // 2), kb // 2), :], own[...]) for i in range(2)], axis=0
    )
    upper_high, upper_low = split(upper)
    upper_both = jnp.concatenate([upper_high, upper_low], axis=1)
    crosses = []
    for i in range(2):
        rows = pl.ds(i * (kb // 2), kb // 2)
        both = dot(sh[rows, :], upper_both)
        crosses.append(-(both[:, :TILE] + both[:, TILE:] + dot(sl[rows, :], upper_high)))
    cross = jnp.concatenate(crosses, axis=0)
    cr[...] = cross
    cross_copy = pltpu.make_async_copy(cr, cross_ref, own_sem.at[0])
    cross_copy.start()
    cross_high, cross_low = split(cross.T)
    stacked = jnp.concatenate([cross_high, cross_low], axis=0)
    turned_copy.wait()
    for copy in lv_copies:
        copy.wait()
    for j in range(pairs):
        rows = pl.ds(wide * j, wide)
        part = dot(stacked, lm[:, rows])
        middle = turned[:, rows].astype(F32) - (part[:TILE] + part[TILE:])
        middle_high, middle_low = split(middle)
        mt[pl.ds(0, TILE), rows] = middle_high
        mt[pl.ds(TILE, TILE), rows] = middle_low
    codes = []
    out_copies = []
    for j in range(pairs):
        rows = pl.ds(wide * j, wide)
        rest_rows = pl.ds(wide * j, ns - wide * j)
        total = dot(mt[:, rest_rows], lv[rest_rows, rows])
        block = (total[:TILE] + total[TILE:]).T
        sg[rows, :] = block
        if first:
            for i in range(2):
                levels, code = code_tile(block[i * TILE : (i + 1) * TILE])
                levels_ref[pl.ds(wide * j + i * TILE, TILE), :] = levels.astype(I16)
                levels_ref[pl.ds(ns + SCALES + (2 * j + i) * HALF, HALF), :] = right_half(
                    levels
                ).astype(I16)
                codes.append(code)
        else:
            copy = pltpu.make_async_copy(sg.at[rows], sigma_ref.at[rows], res_sem.at[j])
            copy.start()
            out_copies.append(copy)
    if first:
        levels_ref[pl.ds(ns, SCALES), :] = (
            jnp.concatenate(codes, axis=0).astype(jnp.int32).astype(I16)
        )
        for p in range(slots_ref.shape[0]):
            moves = [
                (pl.multiple_of(picks_ref[p * SENT + j], SCALES), j * TILE, PIECES[j])
                for j in range(SENT)
            ]
            for j, (start, place, size) in enumerate(moves + [(ns, DATA, SCALES)]):
                copy = pltpu.make_async_copy(
                    levels_ref.at[pl.ds(start, size), :],
                    slots_ref.at[p, pl.ds(place, size), :],
                    out_sem.at[p * (SENT + 1) + j],
                )
                copy.start()
                out_copies.append(copy)
        copy = pltpu.make_async_copy(sg, sigma_ref, res_sem.at[0])
        copy.start()
        out_copies.append(copy)
    cross_copy.wait()
    for copy in out_copies:
        copy.wait()


def solve(tiles, gathered, own, turned, kb, ancestor, slot_tiles=None):
    first = slot_tiles is not None
    blocks = gathered.shape[0]
    ns, width = own.shape
    k = kb // TILE
    outs = [
        jax.ShapeDtypeStruct((ns, width), F32),
        jax.ShapeDtypeStruct((kb, width), F32),
    ]
    parts = sum(len(column_parts(c, blocks, kb)) for c in range(blocks))
    scratch = [
        pltpu.VMEM((kb, ns), BF),
        pltpu.VMEM((ns, ns), BF),
        pltpu.VMEM((ns, width), BF),
        pltpu.VMEM((width, ns), BF),
        pltpu.VMEM((k,) + ancestor.shape[1:], I16),
        pltpu.VMEM((kb, kb), BF),
        pltpu.VMEM((kb, kb), BF),
        pltpu.VMEM((2 * TILE, ns), BF),
        pltpu.VMEM((ns, width), F32),
        pltpu.VMEM((kb, width), F32),
        pltpu.SemaphoreType.DMA((blocks,)),
        pltpu.SemaphoreType.DMA((k,)),
        pltpu.SemaphoreType.DMA((parts,)),
        pltpu.SemaphoreType.DMA((2,)),
        pltpu.SemaphoreType.DMA((blocks // 2,)),
    ]
    operands = [tiles, gathered, own, turned, ancestor]
    in_specs = [SMEM_SPEC, HBM_SPEC, HBM_SPEC, HBM_SPEC, HBM_SPEC]
    if first:
        operands.append(slot_tiles)
        in_specs.append(SMEM_SPEC)
        count = slot_tiles.shape[1]
        outs.append(jax.ShapeDtypeStruct((count, DATA + SCALES, width), I16))
        scratch.append(pltpu.VMEM((ns + SCALES + ns // 2, width), I16))
        scratch.append(pltpu.SMEM((count * SENT,), jnp.int32))
        scratch.append(pltpu.SemaphoreType.DMA((count * (SENT + 1),)))
    return pl.pallas_call(
        functools.partial(solve_kernel, first, blocks, kb),
        out_shape=outs,
        in_specs=in_specs,
        out_specs=[HBM_SPEC] * len(outs),
        scratch_shapes=scratch,
        compiler_params=pltpu.CompilerParams(vmem_limit_bytes=SOLVE_LIMIT),
        cost_estimate=pl.CostEstimate(
            flops=4 * ns * ns * width, transcendentals=0, bytes_accessed=14 << 20
        ),
        name="solve_first" if first else "solve_second",
    )(*operands)


def body(
    sigma_root,
    linv_one,
    panel_one,
    tiles_one,
    mask_one,
    linv_two,
    panel_two,
    tiles_two,
    mask_two,
    parent,
):
    leaf_id = lax.axis_index("leaf")
    kb = panel_one.shape[1]
    ns, width = linv_one.shape[1:]
    blocks = ns // TILE
    cut = (blocks - 1) * TILE // 2
    fold = [(i, blocks - 1 - i) for i in range(blocks)]
    tiles_one, tiles_two = tiles_one.T, tiles_two.T
    mask_one, mask_two = mask_one[0, :, 0], mask_two[0, :, 0]
    source = lax.dynamic_index_in_dim(parent, leaf_id, 0, keepdims=False)

    other_one = lax.ppermute(linv_one[0, :cut], "row", fold)
    coded_one = code(tiles_one, sigma_root)
    turned_one = turn(linv_one[0])
    other_one, later_two = lax.optimization_barrier((other_one, linv_two[0]))
    packed_one = pack(blocks, mask_one, panel_one[0], linv_one[0], other_one)
    packed_one, coded_one, turned_one = lax.optimization_barrier(
        (packed_one, coded_one, turned_one)
    )
    gathered_one = lax.all_gather(packed_one, "row", axis=0)
    other_two = lax.ppermute(later_two[:cut], "row", fold)
    ancestor_one = lax.all_gather(coded_one, "row", axis=0)
    ancestor_one, other_two = lax.optimization_barrier((ancestor_one, other_two))
    turned_two = turn(later_two)
    packed_two = pack(blocks, mask_two, panel_two[0], later_two, other_two)
    gathered_one, packed_two = lax.optimization_barrier((gathered_one, packed_two))
    gathered_two = lax.all_gather(packed_two, "row", axis=0)
    sigma_first, cross_first, slots = solve(
        tiles_one, gathered_one, linv_one[0], turned_one, kb, ancestor_one, tiles_two
    )
    arrived = lax.all_to_all(slots, "leaf", split_axis=0, concat_axis=0, tiled=True)
    chosen = lax.dynamic_index_in_dim(arrived, source, 0, keepdims=False)
    ancestor_two = lax.all_gather(chosen, "row", axis=0)
    sigma_second, cross_second = solve(
        tiles_two, gathered_two, linv_two[0], turned_two, kb, ancestor_two
    )
    return (sigma_first[None], cross_first[None], sigma_second[None], cross_second[None])


def solution(mesh):
    return jax.shard_map(
        body,
        mesh=mesh,
        in_specs=(
            P(None, "row"),
            P("leaf", None, "row"),
            P("leaf", None, "row"),
            P(),
            P("leaf", None, "row"),
            P("leaf", None, "row"),
            P("leaf", None, "row"),
            P(),
            P("leaf", None, "row"),
            P(),
        ),
        out_specs=(
            P("leaf", None, "row"),
            P("leaf", None, "row"),
            P("leaf", None, "row"),
            P("leaf", None, "row"),
        ),
        check_vma=False,
    )
```

```python
import functools

import jax
import jax.numpy as jnp
from jax import lax
from jax.experimental import pallas as pl
from jax.experimental.pallas import tpu as pltpu
from jax.sharding import PartitionSpec as P

TILE = 128
BF = jnp.bfloat16
F32 = jnp.float32
I16 = jnp.int16
VMEM_SPEC = pl.BlockSpec(memory_space=pltpu.VMEM)
SMEM_SPEC = pl.BlockSpec(memory_space=pltpu.SMEM)
HBM_SPEC = pl.BlockSpec(memory_space=pltpu.HBM)
VMEM_LIMIT = 40 << 20
SOLVE_LIMIT = 60 << 20
SENT = 3
HALF = TILE // 2
PIECES = (HALF + HALF // 2, TILE, HALF)
PLACES = (0, PIECES[0], PIECES[0] + PIECES[1])
DATA = sum(PIECES)
SCALES = 16
STEPS = 256.0
TOP = 32512.0


def split(x):
    high = x.astype(BF)
    return high, (x - high.astype(F32)).astype(BF)


def code_tile(x):
    peak = jnp.max(jnp.abs(x), axis=0, keepdims=True)
    code = jnp.clip(jnp.ceil(jnp.log2(peak) * STEPS), -110.0 * STEPS, 127.0 * STEPS)
    levels = jnp.round(x * (TOP / jnp.exp2(code * (1.0 / STEPS))))
    return levels.astype(jnp.int32), code


def right_half(x):
    rows = x.shape[0] // 2
    lane = lax.broadcasted_iota(jnp.int32, (rows, TILE), 1)
    return jnp.where(lane < HALF, pltpu.roll(x[:rows], HALF, 1), x[rows:])


def own_tile(x):
    return jnp.concatenate([x[:HALF], right_half(x[HALF:])], axis=0)


def dot(a, b):
    return jnp.dot(a, b, preferred_element_type=F32)


def sent_tiles(tiles_ref, block, row_id):
    count = tiles_ref.shape[0]
    place = jnp.int32(0)
    for a in range(1, count):
        place = jnp.where(tiles_ref[a, block] == row_id, jnp.int32(a), place)
    picks = []
    for j in range(SENT):
        index = place + j
        picks.append(tiles_ref[jnp.where(index >= count, index - count, index), block])
    return picks, place < count // 2


def code_kernel(tiles_ref, select_ref, out_ref):
    picks, early = sent_tiles(tiles_ref, lax.axis_index("leaf"), lax.axis_index("row"))
    shape = (SCALES, select_ref.shape[1])
    row = lax.broadcasted_iota(jnp.int32, shape, 0)
    codes = jnp.zeros(shape, F32)
    for j in range(SENT):
        start = pl.multiple_of(picks[j] * TILE, TILE)
        levels, code = code_tile(select_ref[pl.ds(start, TILE), :])
        if j == 0:
            levels = own_tile(levels)
        elif j == 2:
            levels = jnp.where(early, right_half(levels), levels[:HALF])
        out_ref[pl.ds(PLACES[j], PIECES[j]), :] = levels.astype(I16)
        codes = jnp.where(row == picks[j], code, codes)
    out_ref[pl.ds(DATA, SCALES), :] = codes.astype(jnp.int32).astype(I16)


def code(tiles, select):
    return pl.pallas_call(
        code_kernel,
        out_shape=jax.ShapeDtypeStruct((DATA + SCALES, select.shape[1]), I16),
        in_specs=[SMEM_SPEC, VMEM_SPEC],
        out_specs=VMEM_SPEC,
        compiler_params=pltpu.CompilerParams(vmem_limit_bytes=VMEM_LIMIT),
        cost_estimate=pl.CostEstimate(flops=1 << 20, transcendentals=0, bytes_accessed=1 << 20),
        name="code",
    )(tiles, select)


def pack_kernel(blocks, mask_ref, panel_ref, linv_ref, other_ref, out_ref):
    kb = panel_ref.shape[0]
    ns = linv_ref.shape[0]
    cut = other_ref.shape[0]
    half = blocks // 2
    row_id = lax.axis_index("row")
    for a in range(kb // TILE):
        rows = pl.ds(a * TILE, TILE)
        weight = mask_ref[a].astype(F32)
        out_ref[rows, :] = (panel_ref[rows, :].astype(F32) * weight).astype(BF)

    @pl.when(row_id < half)
    def _():
        out_ref[pl.ds(kb, ns - cut), :] = linv_ref[pl.ds(cut, ns - cut), :]

    @pl.when(row_id >= half)
    def _():
        out_ref[pl.ds(kb, cut), :] = other_ref[...]
        for i in range(half - 1):

            @pl.when(i < blocks - 1 - row_id)
            def _():
                start = pl.multiple_of(lax.min(row_id + i, blocks - 1) * TILE, TILE)
                out_ref[pl.ds(kb + i * TILE, TILE), :] = linv_ref[pl.ds(start, TILE), :]

        out_ref[pl.ds(kb + cut, TILE), :] = linv_ref[pl.ds(ns - TILE, TILE), :]


def turn_kernel(linv_ref, turned_ref):
    for c in range(linv_ref.shape[0] // TILE):
        rows = pl.ds(c * TILE, TILE)
        turned_ref[:, rows] = linv_ref[rows, :].astype(F32).T.astype(BF)


def turn(linv):
    ns, width = linv.shape
    return pl.pallas_call(
        turn_kernel,
        out_shape=jax.ShapeDtypeStruct((width, ns), BF),
        in_specs=[VMEM_SPEC],
        out_specs=VMEM_SPEC,
        compiler_params=pltpu.CompilerParams(vmem_limit_bytes=VMEM_LIMIT),
        cost_estimate=pl.CostEstimate(
            flops=0, transcendentals=0, bytes_accessed=2 * 2 * ns * width
        ),
        name="turn",
    )(linv)


def pack(blocks, mask, panel, linv, other):
    kb, width = panel.shape
    ns = linv.shape[0]
    rows = kb + ns - other.shape[0]
    return pl.pallas_call(
        functools.partial(pack_kernel, blocks),
        out_shape=jax.ShapeDtypeStruct((rows, width), BF),
        in_specs=[SMEM_SPEC, VMEM_SPEC, VMEM_SPEC, VMEM_SPEC],
        out_specs=VMEM_SPEC,
        compiler_params=pltpu.CompilerParams(vmem_limit_bytes=VMEM_LIMIT),
        cost_estimate=pl.CostEstimate(
            flops=0, transcendentals=0, bytes_accessed=2 * 2 * rows * width
        ),
        name="pack",
    )(mask, panel, linv, other)


def column_parts(c, blocks, kb):
    ns = blocks * TILE
    cut = (blocks - 1) * TILE // 2
    if c < blocks // 2:
        return [
            (c, kb, ns - cut, cut),
            (blocks - 1 - c, kb + TILE * c, cut - TILE * c, TILE * c),
        ]
    parts = [(c, kb + cut, TILE, ns - TILE)]
    if c < blocks - 1:
        parts.append((c, kb, TILE * (blocks - 1 - c), TILE * c))
    return parts


def solve_kernel(first, blocks, kb, tiles_hbm, gath_ref, own_ref, turned_ref, ancestor_ref, *rest):
    if first:
        slot_hbm, sigma_ref, cross_ref, slots_ref = rest[:4]
        rest = rest[4:]
        levels_ref, picks_ref, slot_ref, out_sem = rest[-4:]
    else:
        sigma_ref, cross_ref = rest[:2]
        rest = rest[2:]
    lm, lv, own, turned, raw, sh, sl, mt, sg, cr, lm_sem, s_sem, lv_sem, own_sem, res_sem, tiles_ref = (
        rest[:16]
    )
    ns = blocks * TILE
    wide = 2 * TILE
    pairs = blocks // 2
    k = kb // TILE
    leaf_id = lax.axis_index("leaf")
    tiles_copy = pltpu.make_async_copy(tiles_hbm, tiles_ref, own_sem.at[2])
    tiles_copy.start()
    if first:
        slot_copy = pltpu.make_async_copy(slot_hbm, slot_ref, own_sem.at[3])
        slot_copy.start()
    own_copy = pltpu.make_async_copy(own_ref, own, own_sem.at[0])
    turned_copy = pltpu.make_async_copy(turned_ref, turned, own_sem.at[1])
    lm_copies = [
        pltpu.make_async_copy(
            gath_ref.at[c, pl.ds(0, kb), :], lm.at[:, pl.ds(c * TILE, TILE)], lm_sem.at[c]
        )
        for c in range(blocks)
    ]
    lv_copies = []
    for c in range(blocks):
        for block, start, size, place in column_parts(c, blocks, kb):
            lv_copies.append(
                pltpu.make_async_copy(
                    gath_ref.at[block, pl.ds(start, size), :],
                    lv.at[pl.ds(place, size), pl.ds(c * TILE, TILE)],
                    lv_sem.at[len(lv_copies)],
                )
            )
    for copy in [own_copy] + lm_copies:
        copy.start()
    tiles_copy.wait()
    s_copies = [
        pltpu.make_async_copy(ancestor_ref.at[tiles_ref[b, leaf_id]], raw.at[b], s_sem.at[b])
        for b in range(k)
    ]
    for copy in s_copies + [turned_copy] + lv_copies:
        copy.start()
    for j in range(pairs):
        lv[pl.ds(wide * j, TILE), pl.ds(wide * j + TILE, TILE)] = jnp.zeros((TILE, TILE), BF)
    if first:
        slot_copy.wait()
        row_id = lax.axis_index("row")
        for p in range(slots_ref.shape[0]):
            picks, early = sent_tiles(slot_ref, p, row_id)
            for j, pick in enumerate(picks):
                start = pick * TILE
                if j == 2:
                    start = jnp.where(early, ns + SCALES + PIECES[0] + pick * HALF, start)
                picks_ref[p * SENT + j] = start

    def store(a, b, values):
        high, low = split(values)
        sh[pl.ds(a * TILE, TILE), pl.ds(b * TILE, TILE)] = high
        sl[pl.ds(a * TILE, TILE), pl.ds(b * TILE, TILE)] = low

    for copy in s_copies:
        copy.wait()
    halves = []
    corner = (lax.broadcasted_iota(jnp.int32, (TILE, TILE), 0) >= HALF) & (
        lax.broadcasted_iota(jnp.int32, (TILE, TILE), 1) < HALF
    )
    for b in range(k):
        codes = raw[b, pl.ds(DATA, SCALES), :].astype(jnp.int32).astype(F32)
        code_row = lax.broadcasted_iota(jnp.int32, codes.shape, 0)
        for j in range(SENT):
            a = (b + j) % k
            code = jnp.sum(
                jnp.where(code_row == tiles_ref[a, leaf_id], codes, 0.0), axis=0, keepdims=True
            )
            scale = jnp.exp2(code * (1.0 / STEPS)) * (1.0 / TOP)
            values = raw[b, pl.ds(PLACES[j], PIECES[j]), :].astype(jnp.int32).astype(F32)
            if j == 0:
                low = values[HALF:]
                values = jnp.concatenate([values[:HALF], pltpu.roll(low, HALF, 1), low], axis=0)
                values = values * scale
                store(a, b, jnp.where(corner, values.T, values))
            elif j == 1:
                values = values * scale
                store(a, b, values)
                store(b, a, values.T)
            else:
                if b < k // 2:
                    values = jnp.concatenate([pltpu.roll(values, HALF, 1), values], axis=0)
                halves.append(values * scale)
    for b in range(k // 2):
        a = b + k // 2
        values = jnp.concatenate([halves[a], halves[b].T[HALF:]], axis=0)
        store(b, a, values)
        store(a, b, values.T)
    own_copy.wait()
    for copy in lm_copies:
        copy.wait()
    upper = jnp.concatenate(
        [dot(lm[pl.ds(i * (kb // 2), kb // 2), :], own[...]) for i in range(2)], axis=0
    )
    upper_high, upper_low = split(upper)
    upper_both = jnp.concatenate([upper_high, upper_low], axis=1)
    crosses = []
    for i in range(2):
        rows = pl.ds(i * (kb // 2), kb // 2)
        both = dot(sh[rows, :], upper_both)
        crosses.append(-(both[:, :TILE] + both[:, TILE:] + dot(sl[rows, :], upper_high)))
    cross = jnp.concatenate(crosses, axis=0)
    cr[...] = cross
    cross_copy = pltpu.make_async_copy(cr, cross_ref, own_sem.at[0])
    cross_copy.start()
    cross_high, cross_low = split(cross.T)
    stacked = jnp.concatenate([cross_high, cross_low], axis=0)
    turned_copy.wait()
    for copy in lv_copies:
        copy.wait()
    for j in range(pairs):
        rows = pl.ds(wide * j, wide)
        part = dot(stacked, lm[:, rows])
        middle = turned[:, rows].astype(F32) - (part[:TILE] + part[TILE:])
        middle_high, middle_low = split(middle)
        mt[pl.ds(0, TILE), rows] = middle_high
        mt[pl.ds(TILE, TILE), rows] = middle_low
    codes = []
    out_copies = []
    for j in range(pairs):
        rows = pl.ds(wide * j, wide)
        rest_rows = pl.ds(wide * j, ns - wide * j)
        total = dot(mt[:, rest_rows], lv[rest_rows, rows])
        block = (total[:TILE] + total[TILE:]).T
        sg[rows, :] = block
        if first:
            for i in range(2):
                levels, code = code_tile(block[i * TILE : (i + 1) * TILE])
                levels_ref[pl.ds(wide * j + i * TILE, TILE), :] = levels.astype(I16)
                levels_ref[
                    pl.ds(ns + SCALES + PIECES[0] + (2 * j + i) * HALF, HALF), :
                ] = right_half(
                    levels
                ).astype(I16)
                codes.append(code)
        copy = pltpu.make_async_copy(sg.at[rows], sigma_ref.at[rows], res_sem.at[j])
        copy.start()
        out_copies.append(copy)
    if first:
        own_start = pl.multiple_of(row_id * TILE, TILE)
        levels = levels_ref[pl.ds(own_start, TILE), :].astype(jnp.int32)
        levels_ref[pl.ds(ns + SCALES, PIECES[0]), :] = own_tile(levels).astype(I16)
        levels_ref[pl.ds(ns, SCALES), :] = (
            jnp.concatenate(codes, axis=0).astype(jnp.int32).astype(I16)
        )
        for p in range(slots_ref.shape[0]):
            moves = [(ns + SCALES, PLACES[0], PIECES[0]), (ns, DATA, SCALES)]
            for j in range(1, SENT):
                start = pl.multiple_of(picks_ref[p * SENT + j], SCALES)
                moves.append((start, PLACES[j], PIECES[j]))
            for j, (start, place, size) in enumerate(moves):
                copy = pltpu.make_async_copy(
                    levels_ref.at[pl.ds(start, size), :],
                    slots_ref.at[p, pl.ds(place, size), :],
                    out_sem.at[p * (SENT + 1) + j],
                )
                copy.start()
                out_copies.append(copy)
    cross_copy.wait()
    for copy in out_copies:
        copy.wait()


def solve(tiles, gathered, own, turned, kb, ancestor, slot_tiles=None):
    first = slot_tiles is not None
    blocks = gathered.shape[0]
    ns, width = own.shape
    k = kb // TILE
    outs = [
        jax.ShapeDtypeStruct((ns, width), F32),
        jax.ShapeDtypeStruct((kb, width), F32),
    ]
    parts = sum(len(column_parts(c, blocks, kb)) for c in range(blocks))
    scratch = [
        pltpu.VMEM((kb, ns), BF),
        pltpu.VMEM((ns, ns), BF),
        pltpu.VMEM((ns, width), BF),
        pltpu.VMEM((width, ns), BF),
        pltpu.VMEM((k,) + ancestor.shape[1:], I16),
        pltpu.VMEM((kb, kb), BF),
        pltpu.VMEM((kb, kb), BF),
        pltpu.VMEM((2 * TILE, ns), BF),
        pltpu.VMEM((ns, width), F32),
        pltpu.VMEM((kb, width), F32),
        pltpu.SemaphoreType.DMA((blocks,)),
        pltpu.SemaphoreType.DMA((k,)),
        pltpu.SemaphoreType.DMA((parts,)),
        pltpu.SemaphoreType.DMA((4,)),
        pltpu.SemaphoreType.DMA((blocks // 2,)),
        pltpu.SMEM(tiles.shape, jnp.int32),
    ]
    operands = [tiles, gathered, own, turned, ancestor]
    in_specs = [HBM_SPEC] * 5
    if first:
        operands.append(slot_tiles)
        in_specs.append(HBM_SPEC)
        count = slot_tiles.shape[1]
        outs.append(jax.ShapeDtypeStruct((count, DATA + SCALES, width), I16))
        scratch.append(pltpu.VMEM((ns + SCALES + PIECES[0] + ns // 2, width), I16))
        scratch.append(pltpu.SMEM((count * SENT,), jnp.int32))
        scratch.append(pltpu.SMEM(slot_tiles.shape, jnp.int32))
        scratch.append(pltpu.SemaphoreType.DMA((count * (SENT + 1),)))
    return pl.pallas_call(
        functools.partial(solve_kernel, first, blocks, kb),
        out_shape=outs,
        in_specs=in_specs,
        out_specs=[HBM_SPEC] * len(outs),
        scratch_shapes=scratch,
        compiler_params=pltpu.CompilerParams(vmem_limit_bytes=SOLVE_LIMIT),
        cost_estimate=pl.CostEstimate(
            flops=4 * ns * ns * width, transcendentals=0, bytes_accessed=14 << 20
        ),
        name="solve_first" if first else "solve_second",
    )(*operands)


def body(
    sigma_root,
    linv_one,
    panel_one,
    tiles_one,
    mask_one,
    linv_two,
    panel_two,
    tiles_two,
    mask_two,
    parent,
):
    leaf_id = lax.axis_index("leaf")
    kb = panel_one.shape[1]
    ns, width = linv_one.shape[1:]
    blocks = ns // TILE
    cut = (blocks - 1) * TILE // 2
    fold = [(i, blocks - 1 - i) for i in range(blocks)]
    tiles_one, tiles_two = tiles_one.T, tiles_two.T
    mask_one, mask_two = mask_one[0, :, 0], mask_two[0, :, 0]
    source = lax.dynamic_index_in_dim(parent, leaf_id, 0, keepdims=False)

    other_one = lax.ppermute(linv_one[0, :cut], "row", fold)
    coded_one = code(tiles_one, sigma_root)
    turned_one = turn(linv_one[0])
    other_one, later_two = lax.optimization_barrier((other_one, linv_two[0]))
    packed_one = pack(blocks, mask_one, panel_one[0], linv_one[0], other_one)
    packed_one, coded_one, turned_one = lax.optimization_barrier(
        (packed_one, coded_one, turned_one)
    )
    gathered_one = lax.all_gather(packed_one, "row", axis=0)
    other_two = lax.ppermute(later_two[:cut], "row", fold)
    ancestor_one = lax.all_gather(coded_one, "row", axis=0)
    ancestor_one, other_two = lax.optimization_barrier((ancestor_one, other_two))
    turned_two = turn(later_two)
    packed_two = pack(blocks, mask_two, panel_two[0], later_two, other_two)
    gathered_one, packed_two = lax.optimization_barrier((gathered_one, packed_two))
    gathered_two = lax.all_gather(packed_two, "row", axis=0)
    sigma_first, cross_first, slots = solve(
        tiles_one, gathered_one, linv_one[0], turned_one, kb, ancestor_one, tiles_two
    )
    arrived = lax.all_to_all(slots, "leaf", split_axis=0, concat_axis=0, tiled=True)
    chosen = lax.dynamic_index_in_dim(arrived, source, 0, keepdims=False)
    ancestor_two = lax.all_gather(chosen, "row", axis=0)
    sigma_second, cross_second = solve(
        tiles_two, gathered_two, linv_two[0], turned_two, kb, ancestor_two
    )
    return (sigma_first[None], cross_first[None], sigma_second[None], cross_second[None])


def solution(mesh):
    return jax.shard_map(
        body,
        mesh=mesh,
        in_specs=(
            P(None, "row"),
            P("leaf", None, "row"),
            P("leaf", None, "row"),
            P(),
            P("leaf", None, "row"),
            P("leaf", None, "row"),
            P("leaf", None, "row"),
            P(),
            P("leaf", None, "row"),
            P(),
        ),
        out_specs=(
            P("leaf", None, "row"),
            P("leaf", None, "row"),
            P("leaf", None, "row"),
            P("leaf", None, "row"),
        ),
        check_vma=False,
    )
```

```python
import functools

import jax
import jax.numpy as jnp
from jax import lax
from jax.experimental import pallas as pl
from jax.experimental.pallas import tpu as pltpu
from jax.sharding import PartitionSpec as P

TILE = 128
BF = jnp.bfloat16
F32 = jnp.float32
I16 = jnp.int16
VMEM_SPEC = pl.BlockSpec(memory_space=pltpu.VMEM)
SMEM_SPEC = pl.BlockSpec(memory_space=pltpu.SMEM)
HBM_SPEC = pl.BlockSpec(memory_space=pltpu.HBM)
VMEM_LIMIT = 40 << 20
SOLVE_LIMIT = 60 << 20
SENT = 3
HALF = TILE // 2
PIECES = (HALF + HALF // 2, TILE, HALF)
PLACES = (0, PIECES[0], PIECES[0] + PIECES[1])
DATA = sum(PIECES)
SCALES = 16
STEPS = 256.0
TOP = 32512.0


def split(x):
    high = x.astype(BF)
    return high, (x - high.astype(F32)).astype(BF)


def code_tile(x):
    peak = jnp.max(jnp.abs(x), axis=0, keepdims=True)
    code = jnp.clip(jnp.ceil(jnp.log2(peak) * STEPS), -110.0 * STEPS, 127.0 * STEPS)
    levels = jnp.round(x * (TOP / jnp.exp2(code * (1.0 / STEPS))))
    return levels.astype(jnp.int32), code


def right_half(x):
    rows = x.shape[0] // 2
    lane = lax.broadcasted_iota(jnp.int32, (rows, TILE), 1)
    return jnp.where(lane < HALF, pltpu.roll(x[:rows], HALF, 1), x[rows:])


def own_tile(x):
    return jnp.concatenate([x[:HALF], right_half(x[HALF:])], axis=0)


def dot(a, b):
    return jnp.dot(a, b, preferred_element_type=F32)


def sent_tiles(tiles_ref, block, row_id):
    count = tiles_ref.shape[0]
    place = jnp.int32(0)
    for a in range(1, count):
        place = jnp.where(tiles_ref[a, block] == row_id, jnp.int32(a), place)
    picks = []
    for j in range(SENT):
        index = place + j
        picks.append(tiles_ref[jnp.where(index >= count, index - count, index), block])
    return picks, place < count // 2


def code_kernel(tiles_ref, select_ref, out_ref):
    picks, early = sent_tiles(tiles_ref, lax.axis_index("leaf"), lax.axis_index("row"))
    shape = (SCALES, select_ref.shape[1])
    row = lax.broadcasted_iota(jnp.int32, shape, 0)
    codes = jnp.zeros(shape, F32)
    for j in range(SENT):
        start = pl.multiple_of(picks[j] * TILE, TILE)
        levels, code = code_tile(select_ref[pl.ds(start, TILE), :])
        if j == 0:
            levels = own_tile(levels)
        elif j == 2:
            levels = jnp.where(early, right_half(levels), levels[:HALF])
        out_ref[pl.ds(PLACES[j], PIECES[j]), :] = levels.astype(I16)
        codes = jnp.where(row == picks[j], code, codes)
    out_ref[pl.ds(DATA, SCALES), :] = codes.astype(jnp.int32).astype(I16)


def code(tiles, select):
    return pl.pallas_call(
        code_kernel,
        out_shape=jax.ShapeDtypeStruct((DATA + SCALES, select.shape[1]), I16),
        in_specs=[SMEM_SPEC, VMEM_SPEC],
        out_specs=VMEM_SPEC,
        compiler_params=pltpu.CompilerParams(vmem_limit_bytes=VMEM_LIMIT),
        cost_estimate=pl.CostEstimate(flops=1 << 20, transcendentals=0, bytes_accessed=1 << 20),
        name="code",
    )(tiles, select)


def pack_kernel(blocks, mask_ref, panel_ref, linv_ref, other_ref, out_ref):
    kb = panel_ref.shape[0]
    ns = linv_ref.shape[0]
    cut = other_ref.shape[0]
    half = blocks // 2
    row_id = lax.axis_index("row")
    for a in range(kb // TILE):
        rows = pl.ds(a * TILE, TILE)
        weight = mask_ref[a].astype(F32)
        out_ref[rows, :] = (panel_ref[rows, :].astype(F32) * weight).astype(BF)

    @pl.when(row_id < half)
    def _():
        out_ref[pl.ds(kb, ns - cut), :] = linv_ref[pl.ds(cut, ns - cut), :]

    @pl.when(row_id >= half)
    def _():
        out_ref[pl.ds(kb, cut), :] = other_ref[...]
        for i in range(half - 1):

            @pl.when(i < blocks - 1 - row_id)
            def _():
                start = pl.multiple_of(lax.min(row_id + i, blocks - 1) * TILE, TILE)
                out_ref[pl.ds(kb + i * TILE, TILE), :] = linv_ref[pl.ds(start, TILE), :]

        out_ref[pl.ds(kb + cut, TILE), :] = linv_ref[pl.ds(ns - TILE, TILE), :]


def turn_kernel(linv_ref, turned_ref):
    for c in range(linv_ref.shape[0] // TILE):
        rows = pl.ds(c * TILE, TILE)
        turned_ref[:, rows] = linv_ref[rows, :].astype(F32).T.astype(BF)


def turn(linv):
    ns, width = linv.shape
    return pl.pallas_call(
        turn_kernel,
        out_shape=jax.ShapeDtypeStruct((width, ns), BF),
        in_specs=[VMEM_SPEC],
        out_specs=VMEM_SPEC,
        compiler_params=pltpu.CompilerParams(vmem_limit_bytes=VMEM_LIMIT),
        cost_estimate=pl.CostEstimate(
            flops=0, transcendentals=0, bytes_accessed=2 * 2 * ns * width
        ),
        name="turn",
    )(linv)


def pack(blocks, mask, panel, linv, other):
    kb, width = panel.shape
    ns = linv.shape[0]
    rows = kb + ns - other.shape[0]
    return pl.pallas_call(
        functools.partial(pack_kernel, blocks),
        out_shape=jax.ShapeDtypeStruct((rows, width), BF),
        in_specs=[SMEM_SPEC, VMEM_SPEC, VMEM_SPEC, VMEM_SPEC],
        out_specs=VMEM_SPEC,
        compiler_params=pltpu.CompilerParams(vmem_limit_bytes=VMEM_LIMIT),
        cost_estimate=pl.CostEstimate(
            flops=0, transcendentals=0, bytes_accessed=2 * 2 * rows * width
        ),
        name="pack",
    )(mask, panel, linv, other)


def column_parts(c, blocks, kb):
    ns = blocks * TILE
    cut = (blocks - 1) * TILE // 2
    if c < blocks // 2:
        return [
            (c, kb, ns - cut, cut),
            (blocks - 1 - c, kb + TILE * c, cut - TILE * c, TILE * c),
        ]
    parts = [(c, kb + cut, TILE, ns - TILE)]
    if c < blocks - 1:
        parts.append((c, kb, TILE * (blocks - 1 - c), TILE * c))
    return parts


def solve_kernel(first, blocks, kb, tiles_hbm, gath_ref, own_ref, turned_ref, ancestor_ref, *rest):
    if first:
        slot_hbm, sigma_ref, cross_ref, slots_ref = rest[:4]
        rest = rest[4:]
        levels_ref, picks_ref, slot_ref, out_sem = rest[-4:]
    else:
        sigma_ref, cross_ref = rest[:2]
        rest = rest[2:]
    lm, lv, own, turned, raw, sh, sl, mt, sg, cr, lm_sem, s_sem, lv_sem, own_sem, res_sem, tiles_ref = (
        rest[:16]
    )
    ns = blocks * TILE
    wide = 2 * TILE
    pairs = blocks // 2
    k = kb // TILE
    leaf_id = lax.axis_index("leaf")
    tiles_copy = pltpu.make_async_copy(tiles_hbm, tiles_ref, own_sem.at[2])
    tiles_copy.start()
    if first:
        slot_copy = pltpu.make_async_copy(slot_hbm, slot_ref, own_sem.at[3])
        slot_copy.start()
    own_copy = pltpu.make_async_copy(own_ref, own, own_sem.at[0])
    turned_copy = pltpu.make_async_copy(turned_ref, turned, own_sem.at[1])
    lm_copies = [
        pltpu.make_async_copy(
            gath_ref.at[c, pl.ds(0, kb), :], lm.at[:, pl.ds(c * TILE, TILE)], lm_sem.at[c]
        )
        for c in range(blocks)
    ]
    lv_copies = []
    for c in range(blocks):
        for block, start, size, place in column_parts(c, blocks, kb):
            lv_copies.append(
                pltpu.make_async_copy(
                    gath_ref.at[block, pl.ds(start, size), :],
                    lv.at[pl.ds(place, size), pl.ds(c * TILE, TILE)],
                    lv_sem.at[len(lv_copies)],
                )
            )
    for copy in [own_copy] + lm_copies:
        copy.start()
    tiles_copy.wait()
    s_copies = [
        pltpu.make_async_copy(ancestor_ref.at[tiles_ref[b, leaf_id]], raw.at[b], s_sem.at[b])
        for b in range(k)
    ]
    for copy in s_copies + [turned_copy] + lv_copies:
        copy.start()
    for j in range(pairs):
        lv[pl.ds(wide * j, TILE), pl.ds(wide * j + TILE, TILE)] = jnp.zeros((TILE, TILE), BF)
    if first:
        slot_copy.wait()
        row_id = lax.axis_index("row")
        for p in range(slots_ref.shape[0]):
            picks, early = sent_tiles(slot_ref, p, row_id)
            for j, pick in enumerate(picks):
                start = pick * TILE
                if j == 2:
                    start = jnp.where(early, ns + SCALES + PIECES[0] + pick * HALF, start)
                picks_ref[p * SENT + j] = start

    def store(a, b, values):
        high, low = split(values)
        sh[pl.ds(a * TILE, TILE), pl.ds(b * TILE, TILE)] = high
        sl[pl.ds(a * TILE, TILE), pl.ds(b * TILE, TILE)] = low

    own_copy.wait()
    uppers = [jnp.zeros((kb // 2, TILE), F32) for _ in range(2)]
    for i in range(4):
        for copy in lm_copies[i * 4 : (i + 1) * 4]:
            copy.wait()
        rows = pl.ds(i * 4 * TILE, 4 * TILE)
        for m in range(2):
            part = pl.ds(m * (kb // 2), kb // 2)
            uppers[m] = uppers[m] + dot(lm[part, rows], own[rows, :])
    upper = jnp.concatenate(uppers, axis=0)
    for copy in s_copies:
        copy.wait()
    halves = []
    corner = (lax.broadcasted_iota(jnp.int32, (TILE, TILE), 0) >= HALF) & (
        lax.broadcasted_iota(jnp.int32, (TILE, TILE), 1) < HALF
    )
    for b in range(k):
        codes = raw[b, pl.ds(DATA, SCALES), :].astype(jnp.int32).astype(F32)
        code_row = lax.broadcasted_iota(jnp.int32, codes.shape, 0)
        for j in range(SENT):
            a = (b + j) % k
            code = jnp.sum(
                jnp.where(code_row == tiles_ref[a, leaf_id], codes, 0.0), axis=0, keepdims=True
            )
            scale = jnp.exp2(code * (1.0 / STEPS)) * (1.0 / TOP)
            values = raw[b, pl.ds(PLACES[j], PIECES[j]), :].astype(jnp.int32).astype(F32)
            if j == 0:
                low = values[HALF:]
                values = jnp.concatenate([values[:HALF], pltpu.roll(low, HALF, 1), low], axis=0)
                values = values * scale
                store(a, b, jnp.where(corner, values.T, values))
            elif j == 1:
                values = values * scale
                store(a, b, values)
                store(b, a, values.T)
            else:
                if b < k // 2:
                    values = jnp.concatenate([pltpu.roll(values, HALF, 1), values], axis=0)
                halves.append(values * scale)
    for b in range(k // 2):
        a = b + k // 2
        values = jnp.concatenate([halves[a], halves[b].T[HALF:]], axis=0)
        store(b, a, values)
        store(a, b, values.T)
    upper_high, upper_low = split(upper)
    upper_both = jnp.concatenate([upper_high, upper_low], axis=1)
    crosses = []
    for i in range(2):
        rows = pl.ds(i * (kb // 2), kb // 2)
        both = dot(sh[rows, :], upper_both)
        crosses.append(-(both[:, :TILE] + both[:, TILE:] + dot(sl[rows, :], upper_high)))
    cross = jnp.concatenate(crosses, axis=0)
    cr[...] = cross
    cross_copy = pltpu.make_async_copy(cr, cross_ref, own_sem.at[0])
    cross_copy.start()
    cross_high, cross_low = split(cross.T)
    stacked = jnp.concatenate([cross_high, cross_low], axis=0)
    turned_copy.wait()
    for copy in lv_copies:
        copy.wait()
    for j in range(pairs):
        rows = pl.ds(wide * j, wide)
        part = dot(stacked, lm[:, rows])
        middle = turned[:, rows].astype(F32) - (part[:TILE] + part[TILE:])
        middle_high, middle_low = split(middle)
        mt[pl.ds(0, TILE), rows] = middle_high
        mt[pl.ds(TILE, TILE), rows] = middle_low
    codes = []
    out_copies = []
    for j in range(pairs):
        rows = pl.ds(wide * j, wide)
        rest_rows = pl.ds(wide * j, ns - wide * j)
        total = dot(mt[:, rest_rows], lv[rest_rows, rows])
        block = (total[:TILE] + total[TILE:]).T
        sg[rows, :] = block
        if first:
            for i in range(2):
                levels, code = code_tile(block[i * TILE : (i + 1) * TILE])
                levels_ref[pl.ds(wide * j + i * TILE, TILE), :] = levels.astype(I16)
                levels_ref[
                    pl.ds(ns + SCALES + PIECES[0] + (2 * j + i) * HALF, HALF), :
                ] = right_half(
                    levels
                ).astype(I16)
                codes.append(code)
        copy = pltpu.make_async_copy(sg.at[rows], sigma_ref.at[rows], res_sem.at[j])
        copy.start()
        out_copies.append(copy)
    if first:
        own_start = pl.multiple_of(row_id * TILE, TILE)
        levels = levels_ref[pl.ds(own_start, TILE), :].astype(jnp.int32)
        levels_ref[pl.ds(ns + SCALES, PIECES[0]), :] = own_tile(levels).astype(I16)
        levels_ref[pl.ds(ns, SCALES), :] = (
            jnp.concatenate(codes, axis=0).astype(jnp.int32).astype(I16)
        )
        for p in range(slots_ref.shape[0]):
            moves = [(ns + SCALES, PLACES[0], PIECES[0]), (ns, DATA, SCALES)]
            for j in range(1, SENT):
                start = pl.multiple_of(picks_ref[p * SENT + j], SCALES)
                moves.append((start, PLACES[j], PIECES[j]))
            for j, (start, place, size) in enumerate(moves):
                copy = pltpu.make_async_copy(
                    levels_ref.at[pl.ds(start, size), :],
                    slots_ref.at[p, pl.ds(place, size), :],
                    out_sem.at[p * (SENT + 1) + j],
                )
                copy.start()
                out_copies.append(copy)
    cross_copy.wait()
    for copy in out_copies:
        copy.wait()


def solve(tiles, gathered, own, turned, kb, ancestor, slot_tiles=None):
    first = slot_tiles is not None
    blocks = gathered.shape[0]
    ns, width = own.shape
    k = kb // TILE
    outs = [
        jax.ShapeDtypeStruct((ns, width), F32),
        jax.ShapeDtypeStruct((kb, width), F32),
    ]
    parts = sum(len(column_parts(c, blocks, kb)) for c in range(blocks))
    scratch = [
        pltpu.VMEM((kb, ns), BF),
        pltpu.VMEM((ns, ns), BF),
        pltpu.VMEM((ns, width), BF),
        pltpu.VMEM((width, ns), BF),
        pltpu.VMEM((k,) + ancestor.shape[1:], I16),
        pltpu.VMEM((kb, kb), BF),
        pltpu.VMEM((kb, kb), BF),
        pltpu.VMEM((2 * TILE, ns), BF),
        pltpu.VMEM((ns, width), F32),
        pltpu.VMEM((kb, width), F32),
        pltpu.SemaphoreType.DMA((blocks,)),
        pltpu.SemaphoreType.DMA((k,)),
        pltpu.SemaphoreType.DMA((parts,)),
        pltpu.SemaphoreType.DMA((4,)),
        pltpu.SemaphoreType.DMA((blocks // 2,)),
        pltpu.SMEM(tiles.shape, jnp.int32),
    ]
    operands = [tiles, gathered, own, turned, ancestor]
    in_specs = [HBM_SPEC] * 5
    if first:
        operands.append(slot_tiles)
        in_specs.append(HBM_SPEC)
        count = slot_tiles.shape[1]
        outs.append(jax.ShapeDtypeStruct((count, DATA + SCALES, width), I16))
        scratch.append(pltpu.VMEM((ns + SCALES + PIECES[0] + ns // 2, width), I16))
        scratch.append(pltpu.SMEM((count * SENT,), jnp.int32))
        scratch.append(pltpu.SMEM(slot_tiles.shape, jnp.int32))
        scratch.append(pltpu.SemaphoreType.DMA((count * (SENT + 1),)))
    return pl.pallas_call(
        functools.partial(solve_kernel, first, blocks, kb),
        out_shape=outs,
        in_specs=in_specs,
        out_specs=[HBM_SPEC] * len(outs),
        scratch_shapes=scratch,
        compiler_params=pltpu.CompilerParams(vmem_limit_bytes=SOLVE_LIMIT),
        cost_estimate=pl.CostEstimate(
            flops=4 * ns * ns * width, transcendentals=0, bytes_accessed=14 << 20
        ),
        name="solve_first" if first else "solve_second",
    )(*operands)


def body(
    sigma_root,
    linv_one,
    panel_one,
    tiles_one,
    mask_one,
    linv_two,
    panel_two,
    tiles_two,
    mask_two,
    parent,
):
    leaf_id = lax.axis_index("leaf")
    kb = panel_one.shape[1]
    ns, width = linv_one.shape[1:]
    blocks = ns // TILE
    cut = (blocks - 1) * TILE // 2
    fold = [(i, blocks - 1 - i) for i in range(blocks)]
    tiles_one, tiles_two = tiles_one.T, tiles_two.T
    mask_one, mask_two = mask_one[0, :, 0], mask_two[0, :, 0]
    source = lax.dynamic_index_in_dim(parent, leaf_id, 0, keepdims=False)

    other_one = lax.ppermute(linv_one[0, :cut], "row", fold)
    coded_one = code(tiles_one, sigma_root)
    turned_one = turn(linv_one[0])
    other_one, later_two = lax.optimization_barrier((other_one, linv_two[0]))
    packed_one = pack(blocks, mask_one, panel_one[0], linv_one[0], other_one)
    packed_one, coded_one, turned_one = lax.optimization_barrier(
        (packed_one, coded_one, turned_one)
    )
    gathered_one = lax.all_gather(packed_one, "row", axis=0)
    other_two = lax.ppermute(later_two[:cut], "row", fold)
    ancestor_one = lax.all_gather(coded_one, "row", axis=0)
    ancestor_one, other_two = lax.optimization_barrier((ancestor_one, other_two))
    turned_two = turn(later_two)
    packed_two = pack(blocks, mask_two, panel_two[0], later_two, other_two)
    gathered_two = lax.all_gather(packed_two, "row", axis=0)
    sigma_first, cross_first, slots = solve(
        tiles_one, gathered_one, linv_one[0], turned_one, kb, ancestor_one, tiles_two
    )
    arrived = lax.all_to_all(slots, "leaf", split_axis=0, concat_axis=0, tiled=True)
    chosen = lax.dynamic_index_in_dim(arrived, source, 0, keepdims=False)
    ancestor_two = lax.all_gather(chosen, "row", axis=0)
    sigma_second, cross_second = solve(
        tiles_two, gathered_two, linv_two[0], turned_two, kb, ancestor_two
    )
    return (sigma_first[None], cross_first[None], sigma_second[None], cross_second[None])


def solution(mesh):
    return jax.shard_map(
        body,
        mesh=mesh,
        in_specs=(
            P(None, "row"),
            P("leaf", None, "row"),
            P("leaf", None, "row"),
            P(),
            P("leaf", None, "row"),
            P("leaf", None, "row"),
            P("leaf", None, "row"),
            P(),
            P("leaf", None, "row"),
            P(),
        ),
        out_specs=(
            P("leaf", None, "row"),
            P("leaf", None, "row"),
            P("leaf", None, "row"),
            P("leaf", None, "row"),
        ),
        check_vma=False,
    )
```

```python
import functools

import jax
import jax.numpy as jnp
from jax import lax
from jax.experimental import pallas as pl
from jax.experimental.pallas import tpu as pltpu
from jax.sharding import PartitionSpec as P

TILE = 128
BF = jnp.bfloat16
F32 = jnp.float32
I16 = jnp.int16
VMEM_SPEC = pl.BlockSpec(memory_space=pltpu.VMEM)
SMEM_SPEC = pl.BlockSpec(memory_space=pltpu.SMEM)
HBM_SPEC = pl.BlockSpec(memory_space=pltpu.HBM)
VMEM_LIMIT = 40 << 20
SOLVE_LIMIT = 60 << 20
SENT = 3
HALF = TILE // 2
PIECES = (HALF + HALF // 2, TILE, HALF)
PLACES = (0, PIECES[0], PIECES[0] + PIECES[1])
DATA = sum(PIECES)
SCALES = 16
STEPS = 256.0
TOP = 32512.0


def split(x):
    high = x.astype(BF)
    return high, (x - high.astype(F32)).astype(BF)


def code_tile(x):
    peak = jnp.maximum(jnp.max(jnp.abs(x), axis=0, keepdims=True), 2.0**-110)
    code = jnp.clip(jnp.ceil(jnp.log2(peak) * STEPS), -110.0 * STEPS, 127.0 * STEPS)
    levels = jnp.round(x * (TOP / jnp.exp2(code * (1.0 / STEPS))))
    return levels.astype(jnp.int32), code


def right_half(x):
    rows = x.shape[0] // 2
    lane = lax.broadcasted_iota(jnp.int32, (rows, TILE), 1)
    return jnp.where(lane < HALF, pltpu.roll(x[:rows], HALF, 1), x[rows:])


def own_tile(x):
    return jnp.concatenate([x[:HALF], right_half(x[HALF:])], axis=0)


def dot(a, b):
    return jnp.dot(a, b, preferred_element_type=F32)


def sent_tiles(tiles_ref, block, row_id):
    count = tiles_ref.shape[0]
    place = jnp.int32(0)
    for a in range(1, count):
        place = jnp.where(tiles_ref[a, block] == row_id, jnp.int32(a), place)
    picks = []
    for j in range(SENT):
        index = place + j
        picks.append(tiles_ref[jnp.where(index >= count, index - count, index), block])
    return picks, place < count // 2


def code_kernel(tiles_ref, select_ref, out_ref):
    picks, early = sent_tiles(tiles_ref, lax.axis_index("leaf"), lax.axis_index("row"))
    shape = (SCALES, select_ref.shape[1])
    row = lax.broadcasted_iota(jnp.int32, shape, 0)
    codes = jnp.zeros(shape, F32)
    for j in range(SENT):
        start = pl.multiple_of(picks[j] * TILE, TILE)
        levels, code = code_tile(select_ref[pl.ds(start, TILE), :])
        if j == 0:
            levels = own_tile(levels)
        elif j == 2:
            levels = jnp.where(early, right_half(levels), levels[:HALF])
        out_ref[pl.ds(PLACES[j], PIECES[j]), :] = levels.astype(I16)
        codes = jnp.where(row == picks[j], code, codes)
    out_ref[pl.ds(DATA, SCALES), :] = codes.astype(jnp.int32).astype(I16)


def code(tiles, select):
    return pl.pallas_call(
        code_kernel,
        out_shape=jax.ShapeDtypeStruct((DATA + SCALES, select.shape[1]), I16),
        in_specs=[SMEM_SPEC, VMEM_SPEC],
        out_specs=VMEM_SPEC,
        compiler_params=pltpu.CompilerParams(vmem_limit_bytes=VMEM_LIMIT),
        cost_estimate=pl.CostEstimate(flops=1 << 20, transcendentals=0, bytes_accessed=1 << 20),
        name="code",
    )(tiles, select)


def pack_kernel(blocks, panel_ref, linv_ref, other_ref, out_ref):
    kb = panel_ref.shape[0]
    ns = linv_ref.shape[0]
    cut = other_ref.shape[0]
    half = blocks // 2
    row_id = lax.axis_index("row")
    out_ref[pl.ds(0, kb), :] = panel_ref[...]

    @pl.when(row_id < half)
    def _():
        out_ref[pl.ds(kb, ns - cut), :] = linv_ref[pl.ds(cut, ns - cut), :]

    @pl.when(row_id >= half)
    def _():
        out_ref[pl.ds(kb, cut), :] = other_ref[...]
        for i in range(half - 1):

            @pl.when(i < blocks - 1 - row_id)
            def _():
                start = pl.multiple_of(lax.min(row_id + i, blocks - 1) * TILE, TILE)
                out_ref[pl.ds(kb + i * TILE, TILE), :] = linv_ref[pl.ds(start, TILE), :]

        out_ref[pl.ds(kb + cut, TILE), :] = linv_ref[pl.ds(ns - TILE, TILE), :]


def ready_kernel(mask_ref, panel_ref, linv_ref, masked_ref, turned_ref):
    for a in range(panel_ref.shape[0] // TILE):
        rows = pl.ds(a * TILE, TILE)
        weight = mask_ref[a].astype(F32)
        masked_ref[rows, :] = (panel_ref[rows, :].astype(F32) * weight).astype(BF)
    for c in range(linv_ref.shape[0] // TILE):
        rows = pl.ds(c * TILE, TILE)
        turned_ref[:, rows] = linv_ref[rows, :].astype(F32).T.astype(BF)


def ready(mask, panel, linv):
    ns, width = linv.shape
    return pl.pallas_call(
        ready_kernel,
        out_shape=[
            jax.ShapeDtypeStruct(panel.shape, BF),
            jax.ShapeDtypeStruct((width, ns), BF),
        ],
        in_specs=[SMEM_SPEC, VMEM_SPEC, VMEM_SPEC],
        out_specs=[VMEM_SPEC, VMEM_SPEC],
        compiler_params=pltpu.CompilerParams(vmem_limit_bytes=VMEM_LIMIT),
        cost_estimate=pl.CostEstimate(
            flops=0, transcendentals=0, bytes_accessed=2 * 2 * ns * width
        ),
        name="ready",
    )(mask, panel, linv)


def pack(blocks, panel, linv, other):
    kb, width = panel.shape
    ns = linv.shape[0]
    rows = kb + ns - other.shape[0]
    return pl.pallas_call(
        functools.partial(pack_kernel, blocks),
        out_shape=jax.ShapeDtypeStruct((rows, width), BF),
        in_specs=[VMEM_SPEC, VMEM_SPEC, VMEM_SPEC],
        out_specs=VMEM_SPEC,
        compiler_params=pltpu.CompilerParams(vmem_limit_bytes=VMEM_LIMIT),
        cost_estimate=pl.CostEstimate(
            flops=0, transcendentals=0, bytes_accessed=2 * 2 * rows * width
        ),
        name="pack",
    )(panel, linv, other)


def column_parts(c, blocks, kb):
    ns = blocks * TILE
    cut = (blocks - 1) * TILE // 2
    if c < blocks // 2:
        return [
            (c, kb, ns - cut, cut),
            (blocks - 1 - c, kb + TILE * c, cut - TILE * c, TILE * c),
        ]
    parts = [(c, kb + cut, TILE, ns - TILE)]
    if c < blocks - 1:
        parts.append((c, kb, TILE * (blocks - 1 - c), TILE * c))
    return parts


def solve_kernel(first, blocks, kb, tiles_hbm, gath_ref, own_ref, turned_ref, ancestor_ref, *rest):
    if first:
        slot_hbm, sigma_ref, cross_ref, slots_ref = rest[:4]
        rest = rest[4:]
        levels_ref, picks_ref, slot_ref, out_sem = rest[-4:]
    else:
        sigma_ref, cross_ref = rest[:2]
        rest = rest[2:]
    lm, lv, own, turned, raw, sh, sl, mt, sg, cr, lm_sem, s_sem, lv_sem, own_sem, res_sem, tiles_ref = (
        rest[:16]
    )
    ns = blocks * TILE
    wide = 2 * TILE
    pairs = blocks // 2
    k = kb // TILE
    leaf_id = lax.axis_index("leaf")
    tiles_copy = pltpu.make_async_copy(tiles_hbm, tiles_ref, own_sem.at[2])
    tiles_copy.start()
    if first:
        slot_copy = pltpu.make_async_copy(slot_hbm, slot_ref, own_sem.at[3])
        slot_copy.start()
    own_copy = pltpu.make_async_copy(own_ref, own, own_sem.at[0])
    turned_copy = pltpu.make_async_copy(turned_ref, turned, own_sem.at[1])
    lm_copies = [
        pltpu.make_async_copy(
            gath_ref.at[c, pl.ds(0, kb), :], lm.at[:, pl.ds(c * TILE, TILE)], lm_sem.at[c]
        )
        for c in range(blocks)
    ]
    lv_copies = []
    for c in range(blocks):
        for block, start, size, place in column_parts(c, blocks, kb):
            lv_copies.append(
                pltpu.make_async_copy(
                    gath_ref.at[block, pl.ds(start, size), :],
                    lv.at[pl.ds(place, size), pl.ds(c * TILE, TILE)],
                    lv_sem.at[len(lv_copies)],
                )
            )
    for copy in [own_copy] + lm_copies:
        copy.start()
    tiles_copy.wait()
    s_copies = [
        pltpu.make_async_copy(ancestor_ref.at[tiles_ref[b, leaf_id]], raw.at[b], s_sem.at[b])
        for b in range(k)
    ]
    for copy in s_copies + [turned_copy] + lv_copies:
        copy.start()
    for j in range(pairs):
        lv[pl.ds(wide * j, TILE), pl.ds(wide * j + TILE, TILE)] = jnp.zeros((TILE, TILE), BF)
    if first:
        slot_copy.wait()
        row_id = lax.axis_index("row")
        for p in range(slots_ref.shape[0]):
            picks, early = sent_tiles(slot_ref, p, row_id)
            for j, pick in enumerate(picks):
                start = pick * TILE
                if j == 2:
                    start = jnp.where(early, ns + SCALES + PIECES[0] + pick * HALF, start)
                picks_ref[p * SENT + j] = start

    def store(a, b, values):
        high, low = split(values)
        sh[pl.ds(a * TILE, TILE), pl.ds(b * TILE, TILE)] = high
        sl[pl.ds(a * TILE, TILE), pl.ds(b * TILE, TILE)] = low

    own_copy.wait()
    uppers = [jnp.zeros((kb // 2, TILE), F32) for _ in range(2)]
    for i in range(4):
        for copy in lm_copies[i * 4 : (i + 1) * 4]:
            copy.wait()
        rows = pl.ds(i * 4 * TILE, 4 * TILE)
        for m in range(2):
            part = pl.ds(m * (kb // 2), kb // 2)
            uppers[m] = uppers[m] + dot(lm[part, rows], own[rows, :])
    upper = jnp.concatenate(uppers, axis=0)
    for copy in s_copies:
        copy.wait()
    halves = []
    corner = (lax.broadcasted_iota(jnp.int32, (TILE, TILE), 0) >= HALF) & (
        lax.broadcasted_iota(jnp.int32, (TILE, TILE), 1) < HALF
    )
    for b in range(k):
        codes = raw[b, pl.ds(DATA, SCALES), :].astype(jnp.int32).astype(F32)
        code_row = lax.broadcasted_iota(jnp.int32, codes.shape, 0)
        for j in range(SENT):
            a = (b + j) % k
            code = jnp.sum(
                jnp.where(code_row == tiles_ref[a, leaf_id], codes, 0.0), axis=0, keepdims=True
            )
            scale = jnp.exp2(code * (1.0 / STEPS)) * (1.0 / TOP)
            values = raw[b, pl.ds(PLACES[j], PIECES[j]), :].astype(jnp.int32).astype(F32)
            if j == 0:
                low = values[HALF:]
                values = jnp.concatenate([values[:HALF], pltpu.roll(low, HALF, 1), low], axis=0)
                values = values * scale
                store(a, b, jnp.where(corner, values.T, values))
            elif j == 1:
                values = values * scale
                store(a, b, values)
                store(b, a, values.T)
            else:
                if b < k // 2:
                    values = jnp.concatenate([pltpu.roll(values, HALF, 1), values], axis=0)
                halves.append(values * scale)
    for b in range(k // 2):
        a = b + k // 2
        values = jnp.concatenate([halves[a], halves[b].T[HALF:]], axis=0)
        store(b, a, values)
        store(a, b, values.T)
    upper_high, upper_low = split(upper)
    upper_both = jnp.concatenate([upper_high, upper_low], axis=1)
    crosses = []
    for i in range(2):
        rows = pl.ds(i * (kb // 2), kb // 2)
        both = dot(sh[rows, :], upper_both)
        crosses.append(-(both[:, :TILE] + both[:, TILE:] + dot(sl[rows, :], upper_high)))
    cross = jnp.concatenate(crosses, axis=0)
    cr[...] = cross
    cross_copy = pltpu.make_async_copy(cr, cross_ref, own_sem.at[0])
    cross_copy.start()
    cross_high, cross_low = split(cross.T)
    stacked = jnp.concatenate([cross_high, cross_low], axis=0)
    turned_copy.wait()
    for copy in lv_copies:
        copy.wait()
    for j in range(pairs):
        rows = pl.ds(wide * j, wide)
        part = dot(stacked, lm[:, rows])
        middle = turned[:, rows].astype(F32) - (part[:TILE] + part[TILE:])
        middle_high, middle_low = split(middle)
        mt[pl.ds(0, TILE), rows] = middle_high
        mt[pl.ds(TILE, TILE), rows] = middle_low
    codes = []
    out_copies = []
    for j in range(pairs):
        rows = pl.ds(wide * j, wide)
        rest_rows = pl.ds(wide * j, ns - wide * j)
        total = dot(mt[:, rest_rows], lv[rest_rows, rows])
        block = (total[:TILE] + total[TILE:]).T
        sg[rows, :] = block
        if first:
            for i in range(2):
                levels, code = code_tile(block[i * TILE : (i + 1) * TILE])
                levels_ref[pl.ds(wide * j + i * TILE, TILE), :] = levels.astype(I16)
                levels_ref[
                    pl.ds(ns + SCALES + PIECES[0] + (2 * j + i) * HALF, HALF), :
                ] = right_half(
                    levels
                ).astype(I16)
                codes.append(code)
        copy = pltpu.make_async_copy(sg.at[rows], sigma_ref.at[rows], res_sem.at[j])
        copy.start()
        out_copies.append(copy)
    if first:
        own_start = pl.multiple_of(row_id * TILE, TILE)
        levels = levels_ref[pl.ds(own_start, TILE), :].astype(jnp.int32)
        levels_ref[pl.ds(ns + SCALES, PIECES[0]), :] = own_tile(levels).astype(I16)
        levels_ref[pl.ds(ns, SCALES), :] = (
            jnp.concatenate(codes, axis=0).astype(jnp.int32).astype(I16)
        )
        for p in range(slots_ref.shape[0]):
            moves = [(ns + SCALES, PLACES[0], PIECES[0]), (ns, DATA, SCALES)]
            for j in range(1, SENT):
                start = pl.multiple_of(picks_ref[p * SENT + j], SCALES)
                moves.append((start, PLACES[j], PIECES[j]))
            for j, (start, place, size) in enumerate(moves):
                copy = pltpu.make_async_copy(
                    levels_ref.at[pl.ds(start, size), :],
                    slots_ref.at[p, pl.ds(place, size), :],
                    out_sem.at[p * (SENT + 1) + j],
                )
                copy.start()
                out_copies.append(copy)
    cross_copy.wait()
    for copy in out_copies:
        copy.wait()


def solve(tiles, gathered, own, turned, kb, ancestor, slot_tiles=None):
    first = slot_tiles is not None
    blocks = gathered.shape[0]
    ns, width = own.shape
    k = kb // TILE
    outs = [
        jax.ShapeDtypeStruct((ns, width), F32),
        jax.ShapeDtypeStruct((kb, width), F32),
    ]
    parts = sum(len(column_parts(c, blocks, kb)) for c in range(blocks))
    scratch = [
        pltpu.VMEM((kb, ns), BF),
        pltpu.VMEM((ns, ns), BF),
        pltpu.VMEM((ns, width), BF),
        pltpu.VMEM((width, ns), BF),
        pltpu.VMEM((k,) + ancestor.shape[1:], I16),
        pltpu.VMEM((kb, kb), BF),
        pltpu.VMEM((kb, kb), BF),
        pltpu.VMEM((2 * TILE, ns), BF),
        pltpu.VMEM((ns, width), F32),
        pltpu.VMEM((kb, width), F32),
        pltpu.SemaphoreType.DMA((blocks,)),
        pltpu.SemaphoreType.DMA((k,)),
        pltpu.SemaphoreType.DMA((parts,)),
        pltpu.SemaphoreType.DMA((4,)),
        pltpu.SemaphoreType.DMA((blocks // 2,)),
        pltpu.SMEM(tiles.shape, jnp.int32),
    ]
    operands = [tiles, gathered, own, turned, ancestor]
    in_specs = [HBM_SPEC] * 5
    if first:
        operands.append(slot_tiles)
        in_specs.append(HBM_SPEC)
        count = slot_tiles.shape[1]
        outs.append(jax.ShapeDtypeStruct((count, DATA + SCALES, width), I16))
        scratch.append(pltpu.VMEM((ns + SCALES + PIECES[0] + ns // 2, width), I16))
        scratch.append(pltpu.SMEM((count * SENT,), jnp.int32))
        scratch.append(pltpu.SMEM(slot_tiles.shape, jnp.int32))
        scratch.append(pltpu.SemaphoreType.DMA((count * (SENT + 1),)))
    return pl.pallas_call(
        functools.partial(solve_kernel, first, blocks, kb),
        out_shape=outs,
        in_specs=in_specs,
        out_specs=[HBM_SPEC] * len(outs),
        scratch_shapes=scratch,
        compiler_params=pltpu.CompilerParams(vmem_limit_bytes=SOLVE_LIMIT),
        cost_estimate=pl.CostEstimate(
            flops=4 * ns * ns * width, transcendentals=0, bytes_accessed=14 << 20
        ),
        name="solve_first" if first else "solve_second",
    )(*operands)


def body(
    sigma_root,
    linv_one,
    panel_one,
    tiles_one,
    mask_one,
    linv_two,
    panel_two,
    tiles_two,
    mask_two,
    parent,
):
    leaf_id = lax.axis_index("leaf")
    kb = panel_one.shape[1]
    ns, width = linv_one.shape[1:]
    blocks = ns // TILE
    cut = (blocks - 1) * TILE // 2
    fold = [(i, blocks - 1 - i) for i in range(blocks)]
    tiles_one, tiles_two = tiles_one.T, tiles_two.T
    mask_one, mask_two = mask_one[0, :, 0], mask_two[0, :, 0]
    source = lax.dynamic_index_in_dim(parent, leaf_id, 0, keepdims=False)

    other_one = lax.ppermute(linv_one[0, :cut], "row", fold)
    coded_one = code(tiles_one, sigma_root)
    masked_one, turned_one = ready(mask_one, panel_one[0], linv_one[0])
    other_one, later_two = lax.optimization_barrier((other_one, linv_two[0]))
    packed_one = pack(blocks, masked_one, linv_one[0], other_one)
    packed_one, coded_one, turned_one = lax.optimization_barrier(
        (packed_one, coded_one, turned_one)
    )
    gathered_one = lax.all_gather(packed_one, "row", axis=0)
    other_two = lax.ppermute(later_two[:cut], "row", fold)
    ancestor_one = lax.all_gather(coded_one, "row", axis=0)
    ancestor_one, other_two = lax.optimization_barrier((ancestor_one, other_two))
    masked_two, turned_two = ready(mask_two, panel_two[0], later_two)
    packed_two = pack(blocks, masked_two, later_two, other_two)
    gathered_two = lax.all_gather(packed_two, "row", axis=0)
    sigma_first, cross_first, slots = solve(
        tiles_one, gathered_one, linv_one[0], turned_one, kb, ancestor_one, tiles_two
    )
    arrived = lax.all_to_all(slots, "leaf", split_axis=0, concat_axis=0, tiled=True)
    chosen = lax.dynamic_index_in_dim(arrived, source, 0, keepdims=False)
    ancestor_two = lax.all_gather(chosen, "row", axis=0)
    sigma_second, cross_second = solve(
        tiles_two, gathered_two, linv_two[0], turned_two, kb, ancestor_two
    )
    return (sigma_first[None], cross_first[None], sigma_second[None], cross_second[None])


def solution(mesh):
    return jax.shard_map(
        body,
        mesh=mesh,
        in_specs=(
            P(None, "row"),
            P("leaf", None, "row"),
            P("leaf", None, "row"),
            P(),
            P("leaf", None, "row"),
            P("leaf", None, "row"),
            P("leaf", None, "row"),
            P(),
            P("leaf", None, "row"),
            P(),
        ),
        out_specs=(
            P("leaf", None, "row"),
            P("leaf", None, "row"),
            P("leaf", None, "row"),
            P("leaf", None, "row"),
        ),
        check_vma=False,
    )
```

```python
import functools

import jax
import jax.numpy as jnp
from jax import lax
from jax.experimental import pallas as pl
from jax.experimental.pallas import tpu as pltpu
from jax.sharding import PartitionSpec as P

TILE = 128
BF = jnp.bfloat16
F32 = jnp.float32
I16 = jnp.int16
VMEM_SPEC = pl.BlockSpec(memory_space=pltpu.VMEM)
SMEM_SPEC = pl.BlockSpec(memory_space=pltpu.SMEM)
HBM_SPEC = pl.BlockSpec(memory_space=pltpu.HBM)
VMEM_LIMIT = 40 << 20
SOLVE_LIMIT = 60 << 20
SENT = 3
HALF = TILE // 2
PIECES = (HALF + HALF // 2, TILE, HALF)
PLACES = (0, PIECES[0], PIECES[0] + PIECES[1])
DATA = sum(PIECES)
SCALES = 16
STEPS = 256.0
TOP = 32512.0


def split(x):
    high = x.astype(BF)
    return high, (x - high.astype(F32)).astype(BF)


def code_tile(x):
    peak = jnp.maximum(jnp.max(jnp.abs(x), axis=0, keepdims=True), 2.0**-110)
    code = jnp.clip(jnp.ceil(jnp.log2(peak) * STEPS), -110.0 * STEPS, 127.0 * STEPS)
    levels = jnp.round(x * (TOP / jnp.exp2(code * (1.0 / STEPS))))
    return levels.astype(jnp.int32), code


def right_half(x):
    rows = x.shape[0] // 2
    lane = lax.broadcasted_iota(jnp.int32, (rows, TILE), 1)
    return jnp.where(lane < HALF, pltpu.roll(x[:rows], HALF, 1), x[rows:])


def own_tile(x):
    return jnp.concatenate([x[:HALF], right_half(x[HALF:])], axis=0)


def dot(a, b):
    return jnp.dot(a, b, preferred_element_type=F32)


def sent_tiles(tiles_ref, block, row_id):
    count = tiles_ref.shape[0]
    place = jnp.int32(0)
    for a in range(1, count):
        place = jnp.where(tiles_ref[a, block] == row_id, jnp.int32(a), place)
    picks = []
    for j in range(SENT):
        index = place + j
        picks.append(tiles_ref[jnp.where(index >= count, index - count, index), block])
    return picks, place < count // 2


def code_kernel(tiles_ref, select_ref, out_ref):
    picks, early = sent_tiles(tiles_ref, lax.axis_index("leaf"), lax.axis_index("row"))
    shape = (SCALES, select_ref.shape[1])
    row = lax.broadcasted_iota(jnp.int32, shape, 0)
    codes = jnp.zeros(shape, F32)
    for j in range(SENT):
        start = pl.multiple_of(picks[j] * TILE, TILE)
        levels, code = code_tile(select_ref[pl.ds(start, TILE), :])
        if j == 0:
            levels = own_tile(levels)
        elif j == 2:
            levels = jnp.where(early, right_half(levels), levels[:HALF])
        out_ref[pl.ds(PLACES[j], PIECES[j]), :] = levels.astype(I16)
        codes = jnp.where(row == picks[j], code, codes)
    out_ref[pl.ds(DATA, SCALES), :] = codes.astype(jnp.int32).astype(I16)


def code(tiles, select):
    return pl.pallas_call(
        code_kernel,
        out_shape=jax.ShapeDtypeStruct((DATA + SCALES, select.shape[1]), I16),
        in_specs=[SMEM_SPEC, VMEM_SPEC],
        out_specs=VMEM_SPEC,
        compiler_params=pltpu.CompilerParams(vmem_limit_bytes=VMEM_LIMIT),
        cost_estimate=pl.CostEstimate(flops=1 << 20, transcendentals=0, bytes_accessed=1 << 20),
        name="code",
    )(tiles, select)


def pack_kernel(blocks, panel_ref, linv_ref, other_ref, out_ref):
    kb = panel_ref.shape[0]
    ns = linv_ref.shape[0]
    cut = other_ref.shape[0]
    half = blocks // 2
    row_id = lax.axis_index("row")
    out_ref[pl.ds(0, kb), :] = panel_ref[...]

    @pl.when(row_id < half)
    def _():
        out_ref[pl.ds(kb, ns - cut), :] = linv_ref[pl.ds(cut, ns - cut), :]

    @pl.when(row_id >= half)
    def _():
        out_ref[pl.ds(kb, cut), :] = other_ref[...]
        for i in range(half - 1):

            @pl.when(i < blocks - 1 - row_id)
            def _():
                start = pl.multiple_of(lax.min(row_id + i, blocks - 1) * TILE, TILE)
                out_ref[pl.ds(kb + i * TILE, TILE), :] = linv_ref[pl.ds(start, TILE), :]

        out_ref[pl.ds(kb + cut, TILE), :] = linv_ref[pl.ds(ns - TILE, TILE), :]


def ready_kernel(mask_ref, panel_ref, linv_ref, masked_ref, turned_ref):
    for a in range(panel_ref.shape[0] // TILE):
        rows = pl.ds(a * TILE, TILE)
        weight = mask_ref[a].astype(F32)
        masked_ref[rows, :] = (panel_ref[rows, :].astype(F32) * weight).astype(BF)
    for c in range(linv_ref.shape[0] // TILE):
        rows = pl.ds(c * TILE, TILE)
        turned_ref[:, rows] = linv_ref[rows, :].astype(F32).T.astype(BF)


def ready(mask, panel, linv):
    ns, width = linv.shape
    return pl.pallas_call(
        ready_kernel,
        out_shape=[
            jax.ShapeDtypeStruct(panel.shape, BF),
            jax.ShapeDtypeStruct((width, ns), BF),
        ],
        in_specs=[SMEM_SPEC, VMEM_SPEC, VMEM_SPEC],
        out_specs=[VMEM_SPEC, VMEM_SPEC],
        compiler_params=pltpu.CompilerParams(vmem_limit_bytes=VMEM_LIMIT),
        cost_estimate=pl.CostEstimate(
            flops=0, transcendentals=0, bytes_accessed=2 * 2 * ns * width
        ),
        name="ready",
    )(mask, panel, linv)


def pack(blocks, panel, linv, other):
    kb, width = panel.shape
    ns = linv.shape[0]
    rows = kb + ns - other.shape[0]
    return pl.pallas_call(
        functools.partial(pack_kernel, blocks),
        out_shape=jax.ShapeDtypeStruct((rows, width), BF),
        in_specs=[VMEM_SPEC, VMEM_SPEC, VMEM_SPEC],
        out_specs=VMEM_SPEC,
        compiler_params=pltpu.CompilerParams(vmem_limit_bytes=VMEM_LIMIT),
        cost_estimate=pl.CostEstimate(
            flops=0, transcendentals=0, bytes_accessed=2 * 2 * rows * width
        ),
        name="pack",
    )(panel, linv, other)


def column_parts(c, blocks, kb):
    ns = blocks * TILE
    cut = (blocks - 1) * TILE // 2
    if c < blocks // 2:
        return [
            (c, kb, ns - cut, cut),
            (blocks - 1 - c, kb + TILE * c, cut - TILE * c, TILE * c),
        ]
    parts = [(c, kb + cut, TILE, ns - TILE)]
    if c < blocks - 1:
        parts.append((c, kb, TILE * (blocks - 1 - c), TILE * c))
    return parts


def solve_kernel(first, blocks, kb, tiles_hbm, gath_ref, own_ref, turned_ref, ancestor_ref, *rest):
    if first:
        slot_hbm, sigma_ref, cross_ref, slots_ref = rest[:4]
        rest = rest[4:]
        levels_ref, picks_ref, slot_ref, out_sem = rest[-4:]
    else:
        sigma_ref, cross_ref = rest[:2]
        rest = rest[2:]
    lm, lv, own, turned, raw, sh, sl, mt, sg, cr, lm_sem, s_sem, lv_sem, own_sem, res_sem, tiles_ref = (
        rest[:16]
    )
    ns = blocks * TILE
    wide = 2 * TILE
    pairs = blocks // 2
    k = kb // TILE
    leaf_id = lax.axis_index("leaf")
    tiles_copy = pltpu.make_async_copy(tiles_hbm, tiles_ref, own_sem.at[2])
    tiles_copy.start()
    if first:
        slot_copy = pltpu.make_async_copy(slot_hbm, slot_ref, own_sem.at[3])
        slot_copy.start()
    own_copy = pltpu.make_async_copy(own_ref, own, own_sem.at[0])
    turned_copy = pltpu.make_async_copy(turned_ref, turned, own_sem.at[1])
    lm_copies = [
        pltpu.make_async_copy(
            gath_ref.at[c, pl.ds(0, kb), :], lm.at[:, pl.ds(c * TILE, TILE)], lm_sem.at[c]
        )
        for c in range(blocks)
    ]
    lv_copies = []
    for c in range(blocks):
        for block, start, size, place in column_parts(c, blocks, kb):
            lv_copies.append(
                pltpu.make_async_copy(
                    gath_ref.at[block, pl.ds(start, size), :],
                    lv.at[pl.ds(place, size), pl.ds(c * TILE, TILE)],
                    lv_sem.at[len(lv_copies)],
                )
            )
    for copy in [own_copy] + lm_copies:
        copy.start()
    tiles_copy.wait()
    s_copies = [
        pltpu.make_async_copy(ancestor_ref.at[tiles_ref[b, leaf_id]], raw.at[b], s_sem.at[b])
        for b in range(k)
    ]
    for copy in s_copies + [turned_copy] + lv_copies:
        copy.start()
    for j in range(pairs):
        lv[pl.ds(wide * j, TILE), pl.ds(wide * j + TILE, TILE)] = jnp.zeros((TILE, TILE), BF)
    if first:
        slot_copy.wait()
        row_id = lax.axis_index("row")
        for p in range(slots_ref.shape[0]):
            picks, early = sent_tiles(slot_ref, p, row_id)
            for j, pick in enumerate(picks):
                start = pick * TILE
                if j == 2:
                    start = jnp.where(early, ns + SCALES + PIECES[0] + pick * HALF, start)
                picks_ref[p * SENT + j] = start

    def store(a, b, values):
        high, low = split(values)
        sh[pl.ds(a * TILE, TILE), pl.ds(b * TILE, TILE)] = high
        sl[pl.ds(a * TILE, TILE), pl.ds(b * TILE, TILE)] = low

    own_copy.wait()
    uppers = [jnp.zeros((kb // 2, TILE), F32) for _ in range(2)]
    for i in range(8):
        for copy in lm_copies[i * 2 : (i + 1) * 2]:
            copy.wait()
        rows = pl.ds(i * 2 * TILE, 2 * TILE)
        for m in range(2):
            part = pl.ds(m * (kb // 2), kb // 2)
            uppers[m] = uppers[m] + dot(lm[part, rows], own[rows, :])
    upper = jnp.concatenate(uppers, axis=0)
    for copy in s_copies:
        copy.wait()
    halves = []
    corner = (lax.broadcasted_iota(jnp.int32, (TILE, TILE), 0) >= HALF) & (
        lax.broadcasted_iota(jnp.int32, (TILE, TILE), 1) < HALF
    )
    for b in range(k):
        codes = raw[b, pl.ds(DATA, SCALES), :].astype(jnp.int32).astype(F32)
        code_row = lax.broadcasted_iota(jnp.int32, codes.shape, 0)
        for j in range(SENT):
            a = (b + j) % k
            code = jnp.sum(
                jnp.where(code_row == tiles_ref[a, leaf_id], codes, 0.0), axis=0, keepdims=True
            )
            scale = jnp.exp2(code * (1.0 / STEPS)) * (1.0 / TOP)
            values = raw[b, pl.ds(PLACES[j], PIECES[j]), :].astype(jnp.int32).astype(F32)
            if j == 0:
                low = values[HALF:]
                values = jnp.concatenate([values[:HALF], pltpu.roll(low, HALF, 1), low], axis=0)
                values = values * scale
                store(a, b, jnp.where(corner, values.T, values))
            elif j == 1:
                values = values * scale
                store(a, b, values)
                store(b, a, values.T)
            else:
                if b < k // 2:
                    values = jnp.concatenate([pltpu.roll(values, HALF, 1), values], axis=0)
                halves.append(values * scale)
    for b in range(k // 2):
        a = b + k // 2
        values = jnp.concatenate([halves[a], halves[b].T[HALF:]], axis=0)
        store(b, a, values)
        store(a, b, values.T)
    upper_high, upper_low = split(upper)
    upper_both = jnp.concatenate([upper_high, upper_low], axis=1)
    crosses = []
    for i in range(2):
        rows = pl.ds(i * (kb // 2), kb // 2)
        both = dot(sh[rows, :], upper_both)
        crosses.append(-(both[:, :TILE] + both[:, TILE:] + dot(sl[rows, :], upper_high)))
    cross = jnp.concatenate(crosses, axis=0)
    cr[...] = cross
    cross_copy = pltpu.make_async_copy(cr, cross_ref, own_sem.at[0])
    cross_copy.start()
    cross_high, cross_low = split(cross.T)
    stacked = jnp.concatenate([cross_high, cross_low], axis=0)
    turned_copy.wait()
    for copy in lv_copies:
        copy.wait()
    for j in range(pairs):
        rows = pl.ds(wide * j, wide)
        part = dot(stacked, lm[:, rows])
        middle = turned[:, rows].astype(F32) - (part[:TILE] + part[TILE:])
        middle_high, middle_low = split(middle)
        mt[pl.ds(0, TILE), rows] = middle_high
        mt[pl.ds(TILE, TILE), rows] = middle_low
    codes = []
    out_copies = []
    for j in range(pairs):
        rows = pl.ds(wide * j, wide)
        rest_rows = pl.ds(wide * j, ns - wide * j)
        total = dot(mt[:, rest_rows], lv[rest_rows, rows])
        block = (total[:TILE] + total[TILE:]).T
        sg[rows, :] = block
        if first:
            for i in range(2):
                levels, code = code_tile(block[i * TILE : (i + 1) * TILE])
                levels_ref[pl.ds(wide * j + i * TILE, TILE), :] = levels.astype(I16)
                levels_ref[
                    pl.ds(ns + SCALES + PIECES[0] + (2 * j + i) * HALF, HALF), :
                ] = right_half(
                    levels
                ).astype(I16)
                codes.append(code)
        copy = pltpu.make_async_copy(sg.at[rows], sigma_ref.at[rows], res_sem.at[j])
        copy.start()
        out_copies.append(copy)
    if first:
        own_start = pl.multiple_of(row_id * TILE, TILE)
        levels = levels_ref[pl.ds(own_start, TILE), :].astype(jnp.int32)
        levels_ref[pl.ds(ns + SCALES, PIECES[0]), :] = own_tile(levels).astype(I16)
        levels_ref[pl.ds(ns, SCALES), :] = (
            jnp.concatenate(codes, axis=0).astype(jnp.int32).astype(I16)
        )
        for p in range(slots_ref.shape[0]):
            moves = [(ns + SCALES, PLACES[0], PIECES[0]), (ns, DATA, SCALES)]
            for j in range(1, SENT):
                start = pl.multiple_of(picks_ref[p * SENT + j], SCALES)
                moves.append((start, PLACES[j], PIECES[j]))
            for j, (start, place, size) in enumerate(moves):
                copy = pltpu.make_async_copy(
                    levels_ref.at[pl.ds(start, size), :],
                    slots_ref.at[p, pl.ds(place, size), :],
                    out_sem.at[p * (SENT + 1) + j],
                )
                copy.start()
                out_copies.append(copy)
    cross_copy.wait()
    for copy in out_copies:
        copy.wait()


def solve(tiles, gathered, own, turned, kb, ancestor, slot_tiles=None):
    first = slot_tiles is not None
    blocks = gathered.shape[0]
    ns, width = own.shape
    k = kb // TILE
    outs = [
        jax.ShapeDtypeStruct((ns, width), F32),
        jax.ShapeDtypeStruct((kb, width), F32),
    ]
    parts = sum(len(column_parts(c, blocks, kb)) for c in range(blocks))
    scratch = [
        pltpu.VMEM((kb, ns), BF),
        pltpu.VMEM((ns, ns), BF),
        pltpu.VMEM((ns, width), BF),
        pltpu.VMEM((width, ns), BF),
        pltpu.VMEM((k,) + ancestor.shape[1:], I16),
        pltpu.VMEM((kb, kb), BF),
        pltpu.VMEM((kb, kb), BF),
        pltpu.VMEM((2 * TILE, ns), BF),
        pltpu.VMEM((ns, width), F32),
        pltpu.VMEM((kb, width), F32),
        pltpu.SemaphoreType.DMA((blocks,)),
        pltpu.SemaphoreType.DMA((k,)),
        pltpu.SemaphoreType.DMA((parts,)),
        pltpu.SemaphoreType.DMA((4,)),
        pltpu.SemaphoreType.DMA((blocks // 2,)),
        pltpu.SMEM(tiles.shape, jnp.int32),
    ]
    operands = [tiles, gathered, own, turned, ancestor]
    in_specs = [HBM_SPEC] * 5
    if first:
        operands.append(slot_tiles)
        in_specs.append(HBM_SPEC)
        count = slot_tiles.shape[1]
        outs.append(jax.ShapeDtypeStruct((count, DATA + SCALES, width), I16))
        scratch.append(pltpu.VMEM((ns + SCALES + PIECES[0] + ns // 2, width), I16))
        scratch.append(pltpu.SMEM((count * SENT,), jnp.int32))
        scratch.append(pltpu.SMEM(slot_tiles.shape, jnp.int32))
        scratch.append(pltpu.SemaphoreType.DMA((count * (SENT + 1),)))
    return pl.pallas_call(
        functools.partial(solve_kernel, first, blocks, kb),
        out_shape=outs,
        in_specs=in_specs,
        out_specs=[HBM_SPEC] * len(outs),
        scratch_shapes=scratch,
        compiler_params=pltpu.CompilerParams(vmem_limit_bytes=SOLVE_LIMIT),
        cost_estimate=pl.CostEstimate(
            flops=4 * ns * ns * width, transcendentals=0, bytes_accessed=14 << 20
        ),
        name="solve_first" if first else "solve_second",
    )(*operands)


def body(
    sigma_root,
    linv_one,
    panel_one,
    tiles_one,
    mask_one,
    linv_two,
    panel_two,
    tiles_two,
    mask_two,
    parent,
):
    leaf_id = lax.axis_index("leaf")
    kb = panel_one.shape[1]
    ns, width = linv_one.shape[1:]
    blocks = ns // TILE
    cut = (blocks - 1) * TILE // 2
    fold = [(i, blocks - 1 - i) for i in range(blocks)]
    tiles_one, tiles_two = tiles_one.T, tiles_two.T
    mask_one, mask_two = mask_one[0, :, 0], mask_two[0, :, 0]
    source = lax.dynamic_index_in_dim(parent, leaf_id, 0, keepdims=False)

    other_one = lax.ppermute(linv_one[0, :cut], "row", fold)
    coded_one = code(tiles_one, sigma_root)
    masked_one, turned_one = ready(mask_one, panel_one[0], linv_one[0])
    other_one, later_two = lax.optimization_barrier((other_one, linv_two[0]))
    packed_one = pack(blocks, masked_one, linv_one[0], other_one)
    packed_one, coded_one, turned_one = lax.optimization_barrier(
        (packed_one, coded_one, turned_one)
    )
    gathered_one = lax.all_gather(packed_one, "row", axis=0)
    other_two = lax.ppermute(later_two[:cut], "row", fold)
    ancestor_one = lax.all_gather(coded_one, "row", axis=0)
    ancestor_one, other_two = lax.optimization_barrier((ancestor_one, other_two))
    masked_two, turned_two = ready(mask_two, panel_two[0], later_two)
    packed_two = pack(blocks, masked_two, later_two, other_two)
    gathered_two = lax.all_gather(packed_two, "row", axis=0)
    sigma_first, cross_first, slots = solve(
        tiles_one, gathered_one, linv_one[0], turned_one, kb, ancestor_one, tiles_two
    )
    arrived = lax.all_to_all(slots, "leaf", split_axis=0, concat_axis=0, tiled=True)
    chosen = lax.dynamic_index_in_dim(arrived, source, 0, keepdims=False)
    ancestor_two = lax.all_gather(chosen, "row", axis=0)
    sigma_second, cross_second = solve(
        tiles_two, gathered_two, linv_two[0], turned_two, kb, ancestor_two
    )
    return (sigma_first[None], cross_first[None], sigma_second[None], cross_second[None])


def solution(mesh):
    return jax.shard_map(
        body,
        mesh=mesh,
        in_specs=(
            P(None, "row"),
            P("leaf", None, "row"),
            P("leaf", None, "row"),
            P(),
            P("leaf", None, "row"),
            P("leaf", None, "row"),
            P("leaf", None, "row"),
            P(),
            P("leaf", None, "row"),
            P(),
        ),
        out_specs=(
            P("leaf", None, "row"),
            P("leaf", None, "row"),
            P("leaf", None, "row"),
            P("leaf", None, "row"),
        ),
        check_vma=False,
    )
```
